32 devices in a mesh: seq: 16 (over z, y, core), dp: 2 (over x).
Axes of the slice: x: 2, y: 2, z: 4, core: 2. Of those that a mesh axis runs over, the one named last changes fastest.
Arguments:
- layer_input: bfloat16 [2, 2048, 4096], P('dp', 'seq'), may hold values from -0.3125 to 0.3125
- scan_input: bfloat16 [2, 2048, 2048], P('dp', 'seq'), may hold values from -6 to 6
- readout: bfloat16 [2, 2048, 64], P('dp', 'seq'), may hold values from -6 to 6
- log_decay: float32 [2, 2048, 32], P('dp', 'seq'), may hold values from -1 to 0
- output_cotangent: bfloat16 [2, 2048, 2048], P('dp', 'seq'), may hold values from -0.0078125 to 0.0078125
- write_weight: float32 [4096, 64], P('dp'), may hold values from -6 to 6
- first_moment: float32 [4096, 64], P('dp'), may hold values from -6 to 6
- second_moment: float32 [4096, 64], P('dp'), may hold values from 1 to 25
Outputs:
- decay_gradient: float32 [2, 2048, 32], P('dp', 'seq')
- new_weight: float32 [4096, 64], P('dp')
- new_first: float32 [4096, 64], P('dp')
- new_second: float32 [4096, 64], P('dp')
The draws below stay inside these ranges and needn't reach their ends.
All inputs are finite; a program needn't handle non-finite values.
Results may differ from the reference program's by a relative error of at most 0.0039.
Values may be sent and summed in bfloat16 or wider, within the bound.
A program may use at most 64 MiB of HBM per device.

```python
import math
import jax
import jax.numpy as jnp
from jax import lax

D = 4096
HALF_HEAD_COUNT = 32
HEAD_DIM = 64
STATE = 64
TOK_DEV = 128
SEQUENCE_LENGTH = 2048
BATCH_SEQUENCES = 2


def draw_log_decay(key, part):
    random_keys = jax.random.split(key, 7)
    fast_share = 0.5
    fast_heads = jax.random.uniform(random_keys[0], (HALF_HEAD_COUNT,)) < fast_share
    fast_rate = jnp.exp(jax.random.uniform(random_keys[1], (HALF_HEAD_COUNT,), minval=jnp.log(1.0 / 50.0), maxval=jnp.log(1.0 / 30.0)))
    slow_rate = jnp.exp(jax.random.uniform(random_keys[2], (HALF_HEAD_COUNT,), minval=jnp.log(0.05), maxval=jnp.log(0.5))) / SEQUENCE_LENGTH
    decay_rate = jnp.where(fast_heads, fast_rate, slow_rate)
    roughness = jnp.exp(jax.random.uniform(random_keys[3], (BATCH_SEQUENCES, SEQUENCE_LENGTH, HALF_HEAD_COUNT), minval=-0.7, maxval=0.7))
    block_factor = jnp.exp(jax.random.uniform(random_keys[4], (BATCH_SEQUENCES, SEQUENCE_LENGTH // TOK_DEV, 1, HALF_HEAD_COUNT), minval=-0.7, maxval=0.7))
    block_factor = jnp.broadcast_to(block_factor, (BATCH_SEQUENCES, SEQUENCE_LENGTH // TOK_DEV, TOK_DEV, HALF_HEAD_COUNT)).reshape(BATCH_SEQUENCES, SEQUENCE_LENGTH, HALF_HEAD_COUNT)
    stable_result = -decay_rate[None, None, :] * roughness * block_factor
    spike_location = jax.random.randint(random_keys[5], (BATCH_SEQUENCES, 2, 1), 0, SEQUENCE_LENGTH)
    token_positions = lax.broadcasted_iota(jnp.int32, (BATCH_SEQUENCES, 2, SEQUENCE_LENGTH), 2)
    spike_found = jnp.any(token_positions == spike_location, axis=1)
    spike_loss = jax.random.uniform(random_keys[6], (BATCH_SEQUENCES, SEQUENCE_LENGTH, HALF_HEAD_COUNT), minval=0.2, maxval=0.5)
    final_output = stable_result + jnp.where(spike_found[:, :, None], jnp.log(1.0 - spike_loss), 0.0)
    return final_output.astype(jnp.float32)


def with_spikes(result, own_key, source, target, shards_of, factor):
    owner, partner = [(jnp.arange(result.shape[position]) // (result.shape[position] // shards_of)).reshape([-1 if axis == position else 1 for axis in range(result.ndim)]) for position in (source, target)]
    chosen = jax.random.permutation(own_key, shards_of)[partner]
    strong = (owner == chosen) | (owner == (partner + shards_of // 2) % shards_of)
    return jnp.where(strong, factor * result, result)


def levels(key, extent, cuts, least, largest):
    def one(dim, shards_of):
        heights = jax.random.uniform(jax.random.fold_in(jax.random.fold_in(key, 6), dim), (shards_of,), jnp.float32, least / len(cuts), largest / len(cuts))
        return jnp.repeat(jnp.exp(heights), extent[dim] // shards_of).reshape((-1,) + (1,) * (len(extent) - dim - 1))

    gain = one(*cuts[0])
    for cut in cuts[1:]:
        gain = gain * one(*cut)
    return gain


def centred(rng, extent, deviation, reach, pieces=(), kind=jnp.bfloat16):
    values = deviation * jax.random.normal(rng, extent, jnp.float32)
    if pieces:
        values = values * levels(rng, extent, pieces, -0.22, 0.18)
    return jnp.clip(values, -reach, reach).astype(kind)


def bell_draw_with(own_key, dims, scale, most, cuts, heavy, dtype=jnp.bfloat16):
    values = scale * jax.random.normal(own_key, dims, jnp.float32)
    if cuts:
        values = values * levels(own_key, dims, cuts, -0.22, 0.18)
    return jnp.clip(with_spikes(values, jax.random.fold_in(own_key, 3), *heavy), -most, most).astype(dtype)


def setup_inputs(seed: int = 0) -> dict:
    keys = jax.random.split(jax.random.key(seed), 9)
    layer_input = bell_draw_with(keys[0], (BATCH_SEQUENCES, SEQUENCE_LENGTH, D), 0.015625, 0.3125, ((0, 2), (1, 16)), (0, 2, 2, 2.0))
    scan_input = centred(keys[1], (BATCH_SEQUENCES, SEQUENCE_LENGTH, HALF_HEAD_COUNT * HEAD_DIM), 1.0, 6.0, ((0, 2), (1, 16)))
    readout = centred(keys[2], (BATCH_SEQUENCES, SEQUENCE_LENGTH, STATE), 1.0, 6.0, ((0, 2), (1, 16)))
    log_decay = draw_log_decay(jax.random.fold_in(keys[8], 71), 0)
    output_cotangent = centred(keys[4], (BATCH_SEQUENCES, SEQUENCE_LENGTH, HALF_HEAD_COUNT * HEAD_DIM), (1.0 / SEQUENCE_LENGTH), 0.0078125, ((0, 2), (1, 16)))
    write_weight = centred(keys[5], (D, STATE), 1.0, 6.0, ((0, 2),), jnp.float32)
    first_moment = centred(keys[6], (D, STATE), 1.0, 6.0, ((0, 2),), jnp.float32)
    second_moment = jnp.clip(jnp.exp(math.log(25.0) - 3.218876 * jax.random.uniform(keys[7], (D, STATE), jnp.float32) ** levels(keys[7], (D, STATE), ((0, 2),), -0.2, 0.2)), 1.0, 25.0)
    return {"layer_input": layer_input, "scan_input": scan_input, "readout": readout, "log_decay": log_decay, "output_cotangent": output_cotangent, "write_weight": write_weight, "first_moment": first_moment, "second_moment": second_moment}


beta_one = 0.9
beta_two = 0.999
adam_count = 10.0
learn_rate = 0.01
weight_decay = 0.1
epsilon = 1e-08
highest = lax.Precision.HIGHEST

def block_setup(input_rows, scan_rows, read_rows, decay_rows, back_rows, weight_half):
    length = input_rows.shape[0]
    write_half = jnp.dot(input_rows, weight_half, preferred_element_type=jnp.float32).astype(jnp.bfloat16)
    write_float = lax.optimization_barrier(write_half).astype(jnp.float32)
    running = jnp.cumsum(decay_rows, axis=0)
    overall = running[-1]
    to_end = jnp.exp(overall[None, :] - running)
    from_start = jnp.exp(running)
    scan_heads = scan_rows.astype(jnp.float32).reshape(length, HALF_HEAD_COUNT, HEAD_DIM)
    back_heads = back_rows.astype(jnp.float32).reshape(length, HALF_HEAD_COUNT, HEAD_DIM)
    read_float = read_rows.astype(jnp.float32)
    return (running, overall, to_end, from_start, scan_heads, back_heads, write_float, read_float)

def block_states(input_rows, scan_rows, read_rows, decay_rows, back_rows, weight_half):
    running, overall, to_end, from_start, scan_heads, back_heads, write_float, read_float = block_setup(input_rows, scan_rows, read_rows, decay_rows, back_rows, weight_half)
    state_local = jnp.einsum('shp,sn->hpn', scan_heads * to_end[:, :, None], write_float, precision=highest)
    reverse_local = jnp.einsum('shp,sn->hpn', back_heads * from_start[:, :, None], read_float, precision=highest)
    return (jnp.exp(overall), state_local, reverse_local)

def block_gradients(input_rows, scan_rows, read_rows, decay_rows, back_rows, weight_half, state_before, grad_after):
    length = input_rows.shape[0]
    running, overall, to_end, from_start, scan_heads, back_heads, write_float, read_float = block_setup(input_rows, scan_rows, read_rows, decay_rows, back_rows, weight_half)
    term_one = jnp.exp(overall) * lax.optimization_barrier(jnp.sum(grad_after * state_before, axis=(1, 2)))
    grad_write = jnp.einsum('hpn,sn->shp', grad_after, write_float, precision=highest)
    second_rows = to_end * lax.optimization_barrier(jnp.sum(scan_heads * grad_write, axis=2))
    term_two = jnp.cumsum(second_rows, axis=0) - second_rows
    state_read = jnp.einsum('hpn,sn->shp', state_before, read_float, precision=highest)
    third_rows = from_start * lax.optimization_barrier(jnp.sum(back_heads * state_read, axis=2))
    term_three = jnp.flip(jnp.cumsum(jnp.flip(third_rows, 0), axis=0), 0)
    crossed = jnp.einsum('thp,shp->hts', scan_heads, back_heads, precision=highest)
    heads_running = running.T
    spread = heads_running[:, None, :] - heads_running[:, :, None]
    row_index = lax.broadcasted_iota(jnp.int32, (length, length), 0)
    col_index = lax.broadcasted_iota(jnp.int32, (length, length), 1)
    kernel_mat = jnp.where((row_index <= col_index)[None], jnp.exp(jnp.minimum(spread, 0.0)), 0.0) * crossed
    write_read = jnp.dot(write_float, read_float.T, precision=highest)
    pairing = jnp.where((row_index < col_index)[None], kernel_mat * write_read[None], 0.0)
    balance = (lax.optimization_barrier(jnp.sum(pairing, axis=2)) - lax.optimization_barrier(jnp.sum(pairing, axis=1))).T
    term_four = jnp.cumsum(balance, axis=0) - balance
    decay_grad = term_one[None, :] + term_two + term_three + term_four
    scaled_scan = (scan_heads * to_end[:, :, None]).reshape(length, HALF_HEAD_COUNT * HEAD_DIM)
    write_grad = jnp.dot(scaled_scan, grad_after.reshape(HALF_HEAD_COUNT * HEAD_DIM, STATE), precision=highest)
    write_grad = write_grad + jnp.dot(lax.optimization_barrier(jnp.sum(kernel_mat, axis=0)), read_float, precision=highest)
    write_half = write_grad.astype(jnp.bfloat16)
    partial_grad = jnp.dot(input_rows.T, write_half, preferred_element_type=jnp.float32)
    return (decay_grad, partial_grad)

def one_sequence(weight_half, inputs):
    block_count = SEQUENCE_LENGTH // TOK_DEV

    def to_blocks(array):
        return array.reshape((block_count, TOK_DEV) + array.shape[1:])
    blocked = tuple((to_blocks(array) for array in inputs))

    def states_of(item):
        return block_states(item[0], item[1], item[2], item[3], item[4], weight_half)
    decays, state_local, reverse_local = lax.map(states_of, blocked)
    zero_state = jnp.zeros((HALF_HEAD_COUNT, HEAD_DIM, STATE), jnp.float32)

    def forward_step(running_state, item):
        return (item[0][:, None, None] * running_state + item[1], running_state)
    unused_end, state_before = lax.scan(forward_step, zero_state, (decays, state_local))

    def reverse_step(running_state, item):
        return (item[1] + item[0][:, None, None] * running_state, running_state)
    unused_start, grad_after = lax.scan(reverse_step, zero_state, (decays, reverse_local), reverse=True)

    def grads_of(item):
        return block_gradients(item[0], item[1], item[2], item[3], item[4], weight_half, item[5], item[6])
    decay_grad, partials = lax.map(grads_of, blocked + (state_before, grad_after))
    return (decay_grad.reshape(SEQUENCE_LENGTH, HALF_HEAD_COUNT), lax.optimization_barrier(jnp.sum(partials, axis=0)))

def reference(layer_input, scan_input, readout, log_decay, output_cotangent, write_weight, first_moment, second_moment):
    weight_half = write_weight.astype(jnp.bfloat16)

    def sequence_step(grad_sum, inputs):
        decay_grad, partial_sum = one_sequence(weight_half, inputs)
        return (grad_sum + partial_sum, decay_grad)
    grad_total, decay_gradient = lax.scan(sequence_step, jnp.zeros((D, STATE), jnp.float32), (layer_input, scan_input, readout, log_decay, output_cotangent))
    new_first = beta_one * first_moment + (1.0 - beta_one) * grad_total
    new_second = beta_two * second_moment + (1.0 - beta_two) * grad_total * grad_total
    first_hat = new_first / (1.0 - beta_one ** adam_count)
    second_hat = new_second / (1.0 - beta_two ** adam_count)
    new_weight = write_weight - learn_rate * (first_hat / (jnp.sqrt(second_hat) + epsilon) + weight_decay * write_weight)
    return (decay_gradient, new_weight, new_first, new_second)
```

```python
import functools

import jax
import jax.numpy as jnp
from jax import lax
from jax.experimental import pallas as pl
from jax.experimental.pallas import tpu as pltpu
from jax.sharding import PartitionSpec as P

HEAD_DIM = 64

beta_one = 0.9
beta_two = 0.999
adam_count = 10.0
learn_rate = 0.01
weight_decay = 0.1
epsilon = 1e-08
highest = lax.Precision.HIGHEST
f32 = jnp.float32
bf16 = jnp.bfloat16
MESH = pl.DeviceIdType.MESH
VMEM = pl.BlockSpec(memory_space=pltpu.VMEM)


def remote(src, dst, send_sem, recv_sem, where):
    return pltpu.make_async_remote_copy(
        src_ref=src, dst_ref=dst, send_sem=send_sem, recv_sem=recv_sem, device_id=where,
        device_id_type=MESH,
    )


def loop(low, high, body):
    lax.fori_loop(low, high, lambda i, carry: (body(i), carry)[1], 0)


class Scan:
    def __init__(self, count, me, local, decay, gathered, sent, result, sems):
        self.count, self.me = count, me
        self.local, self.decay, self.gathered, self.sent, self.result = (
            local, decay, gathered, sent, result)
        self.width = local.shape[1] // count
        self.out_send, self.out_recv, self.back_send, self.back_recv = sems

    def columns(self, place):
        return pl.ds(pl.multiple_of(place * self.width, self.width), self.width)

    def outward(self, j, source):
        return remote(self.local.at[:, self.columns(j)], self.gathered.at[source],
                      self.out_send.at[j], self.out_recv.at[source], {"seq": j})

    def homeward(self, i, owner):
        return remote(self.sent.at[i], self.result.at[:, self.columns(owner)],
                      self.back_send.at[i], self.back_recv.at[owner], {"seq": i})

    def start(self):
        loop(1, self.count,
             lambda k: self.outward(lax.rem(self.me + k, self.count), self.me).start())
        self.gathered[self.me] = self.local[:, self.columns(self.me)]

    def combine(self, reverse):
        count, me = self.count, self.me

        def one(k, running):
            i = count - 1 - k if reverse else k

            @pl.when(i != me)
            def _():
                self.outward(i, i).wait_recv()

            self.sent[i] = running.astype(bf16)
            new = self.decay[i] * running + self.gathered[i].astype(f32)

            @pl.when(i != me)
            def _():
                self.homeward(i, me).start()

            return new

        lax.fori_loop(0, count, one, jnp.zeros(self.gathered.shape[1:], f32))
        self.result[:, self.columns(me)] = self.sent[me]

    def finish(self):
        def one(k):
            j = lax.rem(self.me + k, self.count)
            self.outward(j, j).wait_send()
            self.homeward(j, j).wait_send()
            self.homeward(j, j).wait_recv()

        loop(1, self.count, one)


def greet(seq_count, dp_count, same_core):
    seq_me, dp_me = lax.axis_index("seq"), lax.axis_index("dp")
    barrier = pltpu.get_barrier_semaphore()
    loop(1, seq_count, lambda k: pl.semaphore_signal(
        barrier, inc=1, device_id={"seq": lax.rem(seq_me + k, seq_count)}, device_id_type=MESH))
    total = seq_count - 1
    places = seq_count // 2 if same_core else 1

    def over(k):
        d = lax.rem(dp_me + 1 + k // places, dp_count)
        s = lax.rem(seq_me + 2 * (k % places), seq_count)
        pl.semaphore_signal(barrier, inc=1, device_id={"seq": s, "dp": d}, device_id_type=MESH)

    loop(0, (dp_count - 1) * places, over)
    pl.semaphore_wait(barrier, total + (dp_count - 1) * places)


def first_kernel(seq_count, dp_count, weight, local, decay, weights, decays, result,
                 gathered, sent, w_send, w_recv, p_send, p_recv, d_send, d_recv,
                 a_send, a_recv, b_send, b_recv):
    seq_me, dp_me = lax.axis_index("seq"), lax.axis_index("dp")
    core = lax.rem(seq_me, 2)
    partner = seq_me + 1 - 2 * core
    greet(seq_count, dp_count, False)

    def across(d, source):
        return remote(weight.at[core], weights.at[source, core], w_send.at[d], w_recv.at[source],
                      {"dp": d})

    def beside(d, half):
        return remote(weights.at[d, half], weights.at[d, half], p_send.at[d], p_recv.at[d],
                      {"seq": partner})

    def tell(j, source):
        return remote(decay.at[j], decays.at[source], d_send.at[j], d_recv.at[source], {"seq": j})

    loop(1, dp_count, lambda k: across(lax.rem(dp_me + k, dp_count), dp_me).start())
    loop(1, seq_count, lambda k: tell(lax.rem(seq_me + k, seq_count), seq_me).start())
    scan = Scan(seq_count, seq_me, local, decays, gathered, sent, result,
                (a_send, a_recv, b_send, b_recv))
    scan.start()
    decays[seq_me] = decay[seq_me]
    weights[dp_me] = weight[...]

    def told(k):
        j = lax.rem(seq_me + k, seq_count)
        tell(j, j).wait_recv()

    loop(1, seq_count, told)

    def pass_on(k):
        d = lax.rem(dp_me + k, dp_count)
        across(d, d).wait_recv()
        beside(d, core).start()

    loop(1, dp_count, pass_on)
    scan.combine(True)

    def end(k):
        d = lax.rem(dp_me + k, dp_count)
        across(d, d).wait_send()
        beside(d, core).wait_send()
        beside(d, 1 - core).wait_recv()

    loop(1, dp_count, end)
    loop(1, seq_count, lambda k: tell(lax.rem(seq_me + k, seq_count), 0).wait_send())
    scan.finish()


def second_kernel(seq_count, local, decays, result, gathered, sent, a_send, a_recv, b_send, b_recv):
    greet(seq_count, 1, False)
    scan = Scan(seq_count, lax.axis_index("seq"), local, decays, gathered, sent, result,
                (a_send, a_recv, b_send, b_recv))
    scan.start()
    scan.combine(False)
    scan.finish()


def third_kernel(seq_count, dp_count, part, total, halves, summed, pieces,
                 h_send, h_recv, s_send, s_recv, g_send, g_recv):
    seq_me, dp_me = lax.axis_index("seq"), lax.axis_index("dp")
    core = lax.rem(seq_me, 2)
    chip = seq_me // 2
    partner = seq_me + 1 - 2 * core
    group = (seq_count // 2) * dp_count
    mine = chip * dp_count + dp_me
    greet(seq_count, dp_count, True)

    def half(g):
        return remote(part.at[1 - core, g], halves.at[g], h_send.at[g], h_recv.at[g],
                      {"seq": partner})

    def scatter(g, source):
        return remote(summed.at[g], pieces.at[source], s_send.at[g], s_recv.at[source],
                      {"seq": 2 * (g // dp_count) + core, "dp": g % dp_count})

    def share(j, source):
        return remote(total.at[seq_me], total.at[source], g_send.at[j], g_recv.at[source],
                      {"seq": j})

    loop(1, group + 1, lambda k: half(lax.rem(mine + k, group)).start())

    def pair(k):
        g = lax.rem(mine + k, group)
        half(g).wait_recv()
        summed[g] = (part[core, g].astype(f32) + halves[g].astype(f32)).astype(bf16)

        @pl.when(g != mine)
        def _():
            scatter(g, mine).start()

    loop(1, group + 1, pair)

    def collect(k, running):
        g = lax.rem(mine + group - k, group)
        scatter(g, g).wait_recv()
        return running + pieces[g].astype(f32)

    own = part[core, mine].astype(f32) + halves[mine].astype(f32)
    total[seq_me] = lax.fori_loop(1, group, collect, own).astype(bf16)
    loop(1, seq_count, lambda k: share(lax.rem(seq_me + k, seq_count), seq_me).start())

    def end(k):
        j = lax.rem(seq_me + seq_count - k, seq_count)
        share(j, j).wait_recv()
        share(j, j).wait_send()

    loop(1, group + 1, lambda k: half(lax.rem(mine + k, group)).wait_send())
    loop(1, group, lambda k: scatter(lax.rem(mine + k, group), 0).wait_send())
    loop(1, seq_count, end)


def dma(*sizes):
    return [pltpu.SemaphoreType.DMA((size,)) for size in sizes for _ in range(2)]


def adam_update(grad_rows, weight_rows, first_rows, second_rows):
    new_first = beta_one * first_rows + (1.0 - beta_one) * grad_rows
    new_second = beta_two * second_rows + (1.0 - beta_two) * grad_rows * grad_rows
    first_hat = new_first / (1.0 - beta_one**adam_count)
    second_hat = new_second / (1.0 - beta_two**adam_count)
    new_weight = weight_rows - learn_rate * (
        first_hat / (jnp.sqrt(second_hat) + epsilon) + weight_decay * weight_rows
    )
    return (new_weight, new_first, new_second)


def on_device(
    layer_input,
    scan_input,
    readout,
    log_decay,
    output_cotangent,
    write_weight,
    first_moment,
    second_moment,
):
    seq_count, dp_count = lax.axis_size("seq"), lax.axis_size("dp")
    input_rows = layer_input[0]
    scan_rows = scan_input[0]
    read_rows = readout[0]
    decay_rows = log_decay[0]
    back_rows = output_cotangent[0]
    length, model = input_rows.shape
    heads = decay_rows.shape[1]
    channels = scan_rows.shape[1]
    state_size = read_rows.shape[1]
    own_rows = write_weight.shape[0]
    width = channels // seq_count

    running = jnp.cumsum(decay_rows, axis=0)
    overall = running[-1]
    to_end = jnp.exp(overall[None, :] - running)
    from_start = jnp.exp(running)
    decay_total = jnp.exp(overall)

    def widen(a):
        return jnp.repeat(a, HEAD_DIM, axis=1)

    scaled_scan = scan_rows.astype(f32) * widen(to_end)
    scaled_back = back_rows.astype(f32) * widen(from_start)

    def state_of(vectors, rows):
        return lax.dot_general(
            vectors.astype(f32), rows, (((0,), (0,)), ((), ())), precision=highest
        ).astype(bf16)

    reverse_local = state_of(read_rows, scaled_back)
    decay_lanes = widen(decay_total[None]).reshape(seq_count, 1, width)
    weight_half = write_weight.T.astype(bf16).reshape(2, state_size // 2, own_rows)
    exchange = [
        pltpu.VMEM((seq_count, state_size, width), bf16),
        pltpu.VMEM((seq_count, state_size, width), bf16),
    ]
    weights, decays, grad_after = pl.pallas_call(
        functools.partial(first_kernel, seq_count, dp_count),
        out_shape=(
            jax.ShapeDtypeStruct((dp_count,) + weight_half.shape, bf16),
            jax.ShapeDtypeStruct(decay_lanes.shape, f32),
            jax.ShapeDtypeStruct((state_size, channels), bf16),
        ),
        in_specs=[VMEM] * 3,
        out_specs=[VMEM] * 3,
        scratch_shapes=exchange + dma(dp_count, dp_count, seq_count, seq_count, seq_count),
        compiler_params=pltpu.CompilerParams(collective_id=0, has_side_effects=True),
        name="gather_reverse",
    )(weight_half, reverse_local, decay_lanes)

    weight_all = weights.reshape(dp_count, state_size, own_rows).transpose(1, 0, 2)
    write_half = lax.dot_general(
        input_rows, weight_all.reshape(state_size, model), (((1,), (1,)), ((), ())),
        preferred_element_type=f32,
    ).astype(bf16)
    state_local = state_of(write_half, scaled_scan)
    state_before = pl.pallas_call(
        functools.partial(second_kernel, seq_count),
        out_shape=jax.ShapeDtypeStruct((state_size, channels), bf16),
        in_specs=[VMEM] * 2,
        out_specs=VMEM,
        scratch_shapes=exchange + dma(seq_count, seq_count),
        compiler_params=pltpu.CompilerParams(collective_id=1, has_side_effects=True),
        name="forward_states",
    )(state_local, decays)

    scan_split = scan_rows.reshape(length, heads, HEAD_DIM)
    back_split = back_rows.reshape(length, heads, HEAD_DIM)
    crossed = jnp.einsum("thp,shp->hts", scan_split, back_split, preferred_element_type=f32)
    heads_running = running.T
    spread = heads_running[:, None, :] - heads_running[:, :, None]
    row_index = lax.broadcasted_iota(jnp.int32, (length, length), 0)
    col_index = lax.broadcasted_iota(jnp.int32, (length, length), 1)
    kernel_mat = (
        jnp.where((row_index <= col_index)[None], jnp.exp(jnp.minimum(spread, 0.0)), 0.0) * crossed
    )
    kernel_sum = jnp.sum(kernel_mat, axis=0)
    write_grad = jnp.dot(kernel_sum, read_rows.astype(f32), precision=highest)
    write_grad = write_grad + lax.dot_general(
        scaled_scan.astype(bf16), grad_after, (((1,), (1,)), ((), ())), preferred_element_type=f32
    )
    grad_half = write_grad.astype(bf16)
    partial = lax.dot_general(
        grad_half, input_rows, (((0,), (0,)), ((), ())), preferred_element_type=f32
    ).astype(bf16)
    chips = seq_count // 2
    part = partial.reshape(state_size, dp_count, chips, 2, own_rows // seq_count)
    piece = (state_size * own_rows // seq_count // 128, 128)
    part = part.transpose(3, 2, 1, 0, 4).reshape((2, chips * dp_count) + piece)
    grad_sum = pl.pallas_call(
        functools.partial(third_kernel, seq_count, dp_count),
        out_shape=jax.ShapeDtypeStruct((seq_count,) + piece, bf16),
        in_specs=[VMEM],
        out_specs=VMEM,
        scratch_shapes=[pltpu.VMEM((chips * dp_count,) + piece, bf16)] * 3
        + dma(chips * dp_count, chips * dp_count, seq_count),
        compiler_params=pltpu.CompilerParams(collective_id=2, has_side_effects=True),
        name="reduce_gradient",
    )(part)
    grad_rows = grad_sum.reshape(seq_count, state_size, own_rows // seq_count).transpose(1, 0, 2)
    grad_rows = grad_rows.reshape(state_size, own_rows).astype(f32).T
    new_weight, new_first, new_second = adam_update(
        grad_rows, write_weight, first_moment, second_moment
    )

    def per_head(a):
        return jnp.sum(a.reshape(a.shape[0], heads, HEAD_DIM), axis=2)

    term_one = decay_total * jnp.sum(
        per_head(grad_after.astype(f32) * state_before.astype(f32)), axis=0)
    grad_write = jnp.dot(write_half, grad_after, preferred_element_type=f32)
    second_rows = to_end * per_head(scan_rows.astype(f32) * grad_write)
    term_two = jnp.cumsum(second_rows, axis=0) - second_rows
    state_read = jnp.dot(read_rows, state_before, preferred_element_type=f32)
    third_rows = from_start * per_head(back_rows.astype(f32) * state_read)
    term_three = jnp.flip(jnp.cumsum(jnp.flip(third_rows, 0), axis=0), 0)
    write_read = jnp.dot(write_half, read_rows.T, preferred_element_type=f32)
    pairing = jnp.where((row_index < col_index)[None], kernel_mat * write_read[None], 0.0)
    balance = (jnp.sum(pairing, axis=2) - jnp.sum(pairing, axis=1)).T
    term_four = jnp.cumsum(balance, axis=0) - balance
    decay_grad = term_one[None, :] + term_two + term_three + term_four
    return (decay_grad[None], new_weight, new_first, new_second)


def solution(mesh):
    in_specs = (
        P("dp", "seq", None),
        P("dp", "seq", None),
        P("dp", "seq", None),
        P("dp", "seq", None),
        P("dp", "seq", None),
        P("dp", None),
        P("dp", None),
        P("dp", None),
    )
    out_specs = (P("dp", "seq", None), P("dp", None), P("dp", None), P("dp", None))
    return jax.shard_map(
        on_device, mesh=mesh, in_specs=in_specs, out_specs=out_specs, check_vma=False
    )
```

```python
import functools

import jax
import jax.numpy as jnp
from jax import lax
from jax.experimental import pallas as pl
from jax.experimental.pallas import tpu as pltpu
from jax.sharding import PartitionSpec as P

HEAD_DIM = 64

beta_one = 0.9
beta_two = 0.999
adam_count = 10.0
learn_rate = 0.01
weight_decay = 0.1
epsilon = 1e-08
highest = lax.Precision.HIGHEST
f32 = jnp.float32
bf16 = jnp.bfloat16
MESH = pl.DeviceIdType.MESH
VMEM = pl.BlockSpec(memory_space=pltpu.VMEM)


def remote(src, dst, send_sem, recv_sem, where):
    return pltpu.make_async_remote_copy(
        src_ref=src, dst_ref=dst, send_sem=send_sem, recv_sem=recv_sem, device_id=where,
        device_id_type=MESH,
    )


def loop(low, high, body):
    lax.fori_loop(low, high, lambda i, carry: (body(i), carry)[1], 0)


class Scan:
    def __init__(self, count, me, local, decay, gathered, sent, result, sems):
        self.count, self.me = count, me
        self.local, self.decay, self.gathered, self.sent, self.result = (
            local, decay, gathered, sent, result)
        self.width = local.shape[1] // count
        self.out_send, self.out_recv, self.back_send, self.back_recv = sems

    def columns(self, place):
        return pl.ds(pl.multiple_of(place * self.width, self.width), self.width)

    def outward(self, j, source):
        return remote(self.local.at[:, self.columns(j)], self.gathered.at[source],
                      self.out_send.at[j], self.out_recv.at[source], {"seq": j})

    def homeward(self, i, owner):
        return remote(self.sent.at[i], self.result.at[:, self.columns(owner)],
                      self.back_send.at[i], self.back_recv.at[owner], {"seq": i})

    def start(self):
        loop(1, self.count,
             lambda k: self.outward(lax.rem(self.me + k, self.count), self.me).start())
        self.gathered[self.me] = self.local[:, self.columns(self.me)]

    def combine(self, reverse):
        count, me = self.count, self.me

        def one(k, running):
            i = count - 1 - k if reverse else k

            @pl.when(i != me)
            def _():
                self.outward(i, i).wait_recv()

            self.sent[i] = running.astype(bf16)
            new = self.decay[i] * running + self.gathered[i].astype(f32)

            @pl.when(i != me)
            def _():
                self.homeward(i, me).start()

            return new

        lax.fori_loop(0, count, one, jnp.zeros(self.gathered.shape[1:], f32))
        self.result[:, self.columns(me)] = self.sent[me]

    def arrive(self):
        def one(k):
            j = lax.rem(self.me + k, self.count)
            self.homeward(j, j).wait_recv()

        loop(1, self.count, one)

    def drain(self):
        def one(k):
            j = lax.rem(self.me + k, self.count)
            self.outward(j, j).wait_send()
            self.homeward(j, j).wait_send()

        loop(1, self.count, one)

    def finish(self):
        self.arrive()
        self.drain()


def greet(seq_count, dp_count, same_core):
    seq_me, dp_me = lax.axis_index("seq"), lax.axis_index("dp")
    barrier = pltpu.get_barrier_semaphore()
    loop(1, seq_count, lambda k: pl.semaphore_signal(
        barrier, inc=1, device_id={"seq": lax.rem(seq_me + k, seq_count)}, device_id_type=MESH))
    total = seq_count - 1
    places = seq_count // 2 if same_core else 1

    def over(k):
        d = lax.rem(dp_me + 1 + k // places, dp_count)
        s = lax.rem(seq_me + 2 * (k % places), seq_count)
        pl.semaphore_signal(barrier, inc=1, device_id={"seq": s, "dp": d}, device_id_type=MESH)

    loop(0, (dp_count - 1) * places, over)
    return lambda: pl.semaphore_wait(barrier, total + (dp_count - 1) * places)


def first_kernel(seq_count, dp_count, weight, local, decay, weights, decays, result,
                 gathered, sent, w_send, w_recv, p_send, p_recv, d_send, d_recv,
                 a_send, a_recv, b_send, b_recv):
    seq_me, dp_me = lax.axis_index("seq"), lax.axis_index("dp")
    core = lax.rem(seq_me, 2)
    partner = seq_me + 1 - 2 * core
    greet(seq_count, dp_count, False)()

    def across(d, source):
        return remote(weight.at[core], weights.at[source, core], w_send.at[d], w_recv.at[source],
                      {"dp": d})

    def beside(d, half):
        return remote(weights.at[d, half], weights.at[d, half], p_send.at[d], p_recv.at[d],
                      {"seq": partner})

    def tell(j, source):
        return remote(decay.at[j], decays.at[source], d_send.at[j], d_recv.at[source], {"seq": j})

    loop(1, dp_count, lambda k: across(lax.rem(dp_me + k, dp_count), dp_me).start())
    loop(1, seq_count, lambda k: tell(lax.rem(seq_me + k, seq_count), seq_me).start())
    scan = Scan(seq_count, seq_me, local, decays, gathered, sent, result,
                (a_send, a_recv, b_send, b_recv))
    scan.start()
    decays[seq_me] = decay[seq_me]
    weights[dp_me] = weight[...]

    def told(k):
        j = lax.rem(seq_me + k, seq_count)
        tell(j, j).wait_recv()

    loop(1, seq_count, told)

    def pass_on(k):
        d = lax.rem(dp_me + k, dp_count)
        across(d, d).wait_recv()
        beside(d, core).start()

    loop(1, dp_count, pass_on)
    scan.combine(True)

    def end(k):
        d = lax.rem(dp_me + k, dp_count)
        across(d, d).wait_send()
        beside(d, core).wait_send()
        beside(d, 1 - core).wait_recv()

    loop(1, dp_count, end)
    loop(1, seq_count, lambda k: tell(lax.rem(seq_me + k, seq_count), 0).wait_send())
    scan.finish()


def second_kernel(seq_count, local, decays, result, gathered, sent, a_send, a_recv, b_send, b_recv):
    greet(seq_count, 1, False)()
    scan = Scan(seq_count, lax.axis_index("seq"), local, decays, gathered, sent, result,
                (a_send, a_recv, b_send, b_recv))
    scan.start()
    scan.combine(False)
    scan.finish()


def third_kernel(seq_count, dp_count, part, total, halves, summed, pieces,
                 h_send, h_recv, s_send, s_recv, g_send, g_recv):
    seq_me, dp_me = lax.axis_index("seq"), lax.axis_index("dp")
    core = lax.rem(seq_me, 2)
    chip = seq_me // 2
    partner = seq_me + 1 - 2 * core
    group = (seq_count // 2) * dp_count
    mine = chip * dp_count + dp_me
    greet(seq_count, dp_count, True)()

    def half(g):
        return remote(part.at[1 - core, g], halves.at[g], h_send.at[g], h_recv.at[g],
                      {"seq": partner})

    def scatter(g, source):
        return remote(summed.at[g], pieces.at[source], s_send.at[g], s_recv.at[source],
                      {"seq": 2 * (g // dp_count) + core, "dp": g % dp_count})

    def share(j, source):
        return remote(total.at[seq_me], total.at[source], g_send.at[j], g_recv.at[source],
                      {"seq": j})

    loop(1, group + 1, lambda k: half(lax.rem(mine + k, group)).start())

    def pair(k):
        g = lax.rem(mine + k, group)
        half(g).wait_recv()
        summed[g] = (part[core, g].astype(f32) + halves[g].astype(f32)).astype(bf16)

        @pl.when(g != mine)
        def _():
            scatter(g, mine).start()

    loop(1, group + 1, pair)

    def collect(k, running):
        g = lax.rem(mine + group - k, group)
        scatter(g, g).wait_recv()
        return running + pieces[g].astype(f32)

    own = part[core, mine].astype(f32) + halves[mine].astype(f32)
    total[seq_me] = lax.fori_loop(1, group, collect, own).astype(bf16)
    loop(1, seq_count, lambda k: share(lax.rem(seq_me + k, seq_count), seq_me).start())

    def end(k):
        j = lax.rem(seq_me + seq_count - k, seq_count)
        share(j, j).wait_recv()
        share(j, j).wait_send()

    loop(1, group + 1, lambda k: half(lax.rem(mine + k, group)).wait_send())
    loop(1, group, lambda k: scatter(lax.rem(mine + k, group), 0).wait_send())
    loop(1, seq_count, end)


def nt(a, b):
    return lax.dot_general(a, b, (((1,), (1,)), ((), ())), preferred_element_type=f32)


def split(a):
    high = a.astype(bf16)
    return high, (a - high.astype(f32)).astype(bf16)


def exact(a, b):
    return lax.dot_general(a, b, (((1,), (1,)), ((), ())), precision=highest)


def one_kernel(seq_count, dp_count, weight_rows, log_decay, scan_rows, back_rows, read_rows,
               input_rows, decay_grad, total,
               grad_after, state_before, weight, reverse_local, decay, scaled_scan, kernel_mat,
               row_sums, col_sums, weights, decays, forward_local, reverse_got, reverse_sent, forward_got,
               forward_sent, part, halves, summed, pieces,
               w_send, w_recv, p_send, p_recv, d_send, d_recv, a_send, a_recv, b_send, b_recv,
               e_send, e_recv, f_send, f_recv, h_send, h_recv, s_send, s_recv, g_send, g_recv):
    seq_me, dp_me = lax.axis_index("seq"), lax.axis_index("dp")
    core = lax.rem(seq_me, 2)
    chip = seq_me // 2
    partner = seq_me + 1 - 2 * core
    group = (seq_count // 2) * dp_count
    mine = chip * dp_count + dp_me
    ready = greet(seq_count, dp_count, True)
    length, channels = scan_rows.shape
    heads = channels // HEAD_DIM
    state_size = read_rows.shape[0]
    row_index = lax.broadcasted_iota(jnp.int32, (length, length), 0)
    col_index = lax.broadcasted_iota(jnp.int32, (length, length), 1)
    causal = row_index <= col_index
    before = (col_index < row_index).astype(f32)
    upto = (col_index <= row_index).astype(f32)
    onward = causal.astype(f32)
    run_cols = exact(upto, log_decay[...])
    run_rows = exact(log_decay[...], upto)
    overall = run_cols[length - 1 :, :]
    to_end = jnp.exp(overall - run_cols)
    from_start = jnp.exp(run_cols)
    owner = lax.broadcasted_iota(jnp.int32, (heads, channels), 0)
    spot = lax.broadcasted_iota(jnp.int32, (heads, channels), 1) - owner * HEAD_DIM
    member = ((spot >= 0) & (spot < HEAD_DIM)).astype(bf16)

    def widen(a):
        high, low = split(a)
        return (jnp.dot(high, member, preferred_element_type=f32)
                + jnp.dot(low, member, preferred_element_type=f32))

    def per_head(a):
        high, low = split(a)
        return nt(high, member) + nt(low, member)

    back_high, back_low = split(back_rows[...].astype(f32) * widen(from_start))
    reverse_local[...] = (
        jnp.dot(read_rows[...], back_high, preferred_element_type=f32)
        + jnp.dot(read_rows[...], back_low, preferred_element_type=f32)
    ).astype(bf16)
    decay_wide = widen(jnp.exp(jnp.broadcast_to(overall, (8, heads))))[:1]
    width = channels // seq_count
    for j in range(seq_count):
        decay[j] = decay_wide[:, j * width : (j + 1) * width]
    for side in range(2):
        weight[side] = weight_rows[
            side * state_size // 2 : (side + 1) * state_size // 2, :].astype(bf16)
    ready()

    def across(d, source):
        return remote(weight.at[core], weights.at[source, core], w_send.at[d], w_recv.at[source],
                      {"dp": d})

    def beside(d, half):
        return remote(weights.at[d, half], weights.at[d, half], p_send.at[d], p_recv.at[d],
                      {"seq": partner})

    def tell(j, source):
        return remote(decay.at[j], decays.at[source], d_send.at[j], d_recv.at[source], {"seq": j})

    def half(g):
        return remote(part.at[1 - core, g], halves.at[g], h_send.at[g], h_recv.at[g],
                      {"seq": partner})

    def scatter(g, source):
        return remote(summed.at[g], pieces.at[source], s_send.at[g], s_recv.at[source],
                      {"seq": 2 * (g // dp_count) + core, "dp": g % dp_count})

    def share(j, source):
        return remote(total.at[seq_me], total.at[source], g_send.at[j], g_recv.at[source],
                      {"seq": j})

    loop(1, dp_count, lambda k: across(lax.rem(dp_me + k, dp_count), dp_me).start())
    loop(1, seq_count, lambda k: tell(lax.rem(seq_me + k, seq_count), seq_me).start())
    reverse = Scan(seq_count, seq_me, reverse_local, decays, reverse_got, reverse_sent, grad_after,
                   (a_send, a_recv, b_send, b_recv))
    forward = Scan(seq_count, seq_me, forward_local, decays, forward_got, forward_sent,
                   state_before, (e_send, e_recv, f_send, f_recv))
    reverse.start()
    decays[seq_me] = decay[seq_me]
    weights[dp_me] = weight[...]

    kernel_sum = jnp.zeros((length, length), f32)
    scaled_scan[...] = scan_rows[...].astype(f32) * widen(to_end)
    for h in range(heads):
        at = slice(h * HEAD_DIM, (h + 1) * HEAD_DIM)
        crossed = nt(scan_rows[:, at], back_rows[:, at])
        spread = run_rows[h : h + 1, :] - run_cols[:, h : h + 1]
        term = jnp.where(causal, jnp.exp(jnp.minimum(spread, 0.0)), 0.0) * crossed
        kernel_mat[h] = term
        kernel_sum += term

    def pass_on(k):
        d = lax.rem(dp_me + k, dp_count)
        across(d, d).wait_recv()
        beside(d, core).start()

    def told(k):
        j = lax.rem(seq_me + k, seq_count)
        tell(j, j).wait_recv()

    loop(1, dp_count, pass_on)
    loop(1, seq_count, told)
    reverse.combine(True)

    def beside_end(k):
        d = lax.rem(dp_me + k, dp_count)
        beside(d, 1 - core).wait_recv()

    loop(1, dp_count, beside_end)
    own_rows = weight.shape[2]
    write = []
    for side in range(2):
        some = nt(weights[0, side], input_rows[:, :own_rows])
        for d in range(1, dp_count):
            some += nt(weights[d, side], input_rows[:, d * own_rows : (d + 1) * own_rows])
        write.append(some)
    write = jnp.concatenate(write, axis=0)
    write_rows = write.T.astype(bf16)
    write = write.astype(bf16)
    step = channels // 4
    for low in range(0, channels, step):
        scan_high, scan_low = split(scaled_scan[:, low : low + step])
        forward_local[:, low : low + step] = (
            jnp.dot(write, scan_high, preferred_element_type=f32)
            + jnp.dot(write, scan_low, preferred_element_type=f32)
        ).astype(bf16)
    forward.start()

    reverse.arrive()
    sum_high, sum_low = split(kernel_sum)
    write_grad = nt(grad_after[...], scaled_scan[...].astype(bf16))
    write_grad += nt(read_rows[...], sum_high) + nt(read_rows[...], sum_low)
    grad_half = write_grad.astype(bf16)
    wide = own_rows // seq_count
    for g in range(group):
        low = (g % dp_count) * own_rows + 2 * (g // dp_count) * wide
        term = jnp.dot(grad_half, input_rows[:, low : low + 2 * wide],
                       preferred_element_type=f32).astype(bf16)
        part[0, g] = term[:, :wide]
        part[1, g] = term[:, wide:]
    loop(1, group + 1, lambda k: half(lax.rem(mine + k, group)).start())
    forward.combine(False)

    def pair(k):
        g = lax.rem(mine + k, group)
        half(g).wait_recv()
        summed[g] = (part[core, g].astype(f32) + halves[g].astype(f32)).astype(bf16)

        @pl.when(g != mine)
        def _():
            scatter(g, mine).start()

    loop(1, group + 1, pair)

    read_turned = read_rows[...].astype(f32).T.astype(bf16)
    write_read = jnp.where(row_index < col_index, nt(write_rows, read_turned), 0.0)
    for h in range(heads):
        pairing = kernel_mat[h] * write_read
        row_sums[:, h : h + 1] = jnp.sum(pairing, axis=1, keepdims=True)
        col_sums[h : h + 1, :] = jnp.sum(pairing, axis=0, keepdims=True)
    grad_write = jnp.dot(write_rows, grad_after[...], preferred_element_type=f32)
    second = to_end * per_head(scan_rows[...].astype(f32) * grad_write) + row_sums[...]

    def collect(k, running):
        g = lax.rem(mine + group - k, group)
        scatter(g, g).wait_recv()
        return running + pieces[g].astype(f32)

    own = part[core, mine].astype(f32) + halves[mine].astype(f32)
    total[seq_me] = lax.fori_loop(1, group, collect, own).astype(bf16)
    loop(1, seq_count, lambda k: share(lax.rem(seq_me + k, seq_count), seq_me).start())
    forward.arrive()
    state_read = jnp.dot(read_turned, state_before[...], preferred_element_type=f32)
    third = from_start * per_head(back_rows[...].astype(f32) * state_read)
    both = jnp.sum(grad_after[...].astype(f32) * state_before[...].astype(f32), axis=0,
                   keepdims=True)
    first = jnp.exp(overall) * per_head(jnp.broadcast_to(both, (8, channels)))[:1]
    decay_grad[...] = (
        first
        + jnp.dot(before, second, precision=highest)
        - exact(before, col_sums[...])
        + jnp.dot(onward, third, precision=highest)
    )

    def end(k):
        j = lax.rem(seq_me + seq_count - k, seq_count)
        share(j, j).wait_recv()
        share(j, j).wait_send()
        tell(j, j).wait_send()

    def dp_end(k):
        d = lax.rem(dp_me + k, dp_count)
        across(d, d).wait_send()
        beside(d, core).wait_send()

    loop(1, dp_count, dp_end)
    reverse.drain()
    forward.drain()
    loop(1, group + 1, lambda k: half(lax.rem(mine + k, group)).wait_send())
    loop(1, group, lambda k: scatter(lax.rem(mine + k, group), 0).wait_send())
    loop(1, seq_count, end)


def dma(*sizes):
    return [pltpu.SemaphoreType.DMA((size,)) for size in sizes for _ in range(2)]


def adam_update(grad_rows, weight_rows, first_rows, second_rows):
    new_first = beta_one * first_rows + (1.0 - beta_one) * grad_rows
    new_second = beta_two * second_rows + (1.0 - beta_two) * grad_rows * grad_rows
    first_hat = new_first / (1.0 - beta_one**adam_count)
    second_hat = new_second / (1.0 - beta_two**adam_count)
    new_weight = weight_rows - learn_rate * (
        first_hat / (jnp.sqrt(second_hat) + epsilon) + weight_decay * weight_rows
    )
    return (new_weight, new_first, new_second)


def on_device(
    layer_input,
    scan_input,
    readout,
    log_decay,
    output_cotangent,
    write_weight,
    first_moment,
    second_moment,
):
    seq_count, dp_count = lax.axis_size("seq"), lax.axis_size("dp")
    input_rows = layer_input[0]
    scan_rows = scan_input[0]
    read_rows = readout[0]
    decay_rows = log_decay[0]
    back_rows = output_cotangent[0]
    length, model = input_rows.shape
    heads = decay_rows.shape[1]
    channels = scan_rows.shape[1]
    state_size = read_rows.shape[1]
    own_rows = write_weight.shape[0]
    width = channels // seq_count

    chips = seq_count // 2
    group = chips * dp_count
    if own_rows % (128 * seq_count) == 0:
        piece = (state_size, own_rows // seq_count)
        exchange = [pltpu.VMEM((seq_count, state_size, width), bf16)] * 2
        states = pltpu.VMEM((state_size, channels), bf16)
        halves = (2, state_size // 2, own_rows)
        decay_grad, grad_sum = pl.pallas_call(
            functools.partial(one_kernel, seq_count, dp_count),
            out_shape=(
                jax.ShapeDtypeStruct((length, heads), f32),
                jax.ShapeDtypeStruct((seq_count,) + piece, bf16),
            ),
            in_specs=[VMEM] * 6,
            out_specs=[VMEM] * 2,
            scratch_shapes=[
                states,
                states,
                pltpu.VMEM(halves, bf16),
                states,
                pltpu.VMEM((seq_count, 1, width), f32),
                pltpu.VMEM((length, channels), f32),
                pltpu.VMEM((heads, length, length), f32),
                pltpu.VMEM((length, heads), f32),
                pltpu.VMEM((heads, length), f32),
                pltpu.VMEM((dp_count,) + halves, bf16),
                pltpu.VMEM((seq_count, 1, width), f32),
                states,
            ]
            + exchange
            + exchange
            + [pltpu.VMEM((2, group) + piece, bf16)]
            + [pltpu.VMEM((group,) + piece, bf16)] * 3
            + dma(dp_count, dp_count, seq_count, seq_count, seq_count, seq_count, seq_count,
                  group, group, seq_count),
            compiler_params=pltpu.CompilerParams(collective_id=3, has_side_effects=True),
            name="whole_step",
        )(write_weight.T, decay_rows.T, scan_rows, back_rows, read_rows.T, input_rows)
    else:
        running = jnp.cumsum(decay_rows, axis=0)
        overall = running[-1]
        to_end = jnp.exp(overall[None, :] - running)
        from_start = jnp.exp(running)
        decay_total = jnp.exp(overall)

        def widen(a):
            return jnp.repeat(a, HEAD_DIM, axis=1)

        scaled_scan = scan_rows.astype(f32) * widen(to_end)
        scaled_back = back_rows.astype(f32) * widen(from_start)

        def state_of(vectors, rows):
            return lax.dot_general(
                vectors.astype(f32), rows, (((0,), (0,)), ((), ())), precision=highest
            ).astype(bf16)

        reverse_local = state_of(read_rows, scaled_back)
        decay_lanes = widen(decay_total[None]).reshape(seq_count, 1, width)
        weight_half = write_weight.T.astype(bf16).reshape(2, state_size // 2, own_rows)
        exchange = [
            pltpu.VMEM((seq_count, state_size, width), bf16),
            pltpu.VMEM((seq_count, state_size, width), bf16),
        ]
        piece = (state_size * own_rows // seq_count // 128, 128)
        scan_split = scan_rows.reshape(length, heads, HEAD_DIM)
        back_split = back_rows.reshape(length, heads, HEAD_DIM)
        crossed = jnp.einsum("thp,shp->hts", scan_split, back_split, preferred_element_type=f32)
        heads_running = running.T
        spread = heads_running[:, None, :] - heads_running[:, :, None]
        row_index = lax.broadcasted_iota(jnp.int32, (length, length), 0)
        col_index = lax.broadcasted_iota(jnp.int32, (length, length), 1)
        kernel_mat = (
            jnp.where((row_index <= col_index)[None], jnp.exp(jnp.minimum(spread, 0.0)), 0.0) * crossed
        )
        weights, decays, grad_after = pl.pallas_call(
            functools.partial(first_kernel, seq_count, dp_count),
            out_shape=(
                jax.ShapeDtypeStruct((dp_count,) + weight_half.shape, bf16),
                jax.ShapeDtypeStruct(decay_lanes.shape, f32),
                jax.ShapeDtypeStruct((state_size, channels), bf16),
            ),
            in_specs=[VMEM] * 3,
            out_specs=[VMEM] * 3,
            scratch_shapes=exchange + dma(dp_count, dp_count, seq_count, seq_count, seq_count),
            compiler_params=pltpu.CompilerParams(collective_id=0, has_side_effects=True),
            name="gather_reverse",
        )(weight_half, reverse_local, decay_lanes)

        weight_all = weights.reshape(dp_count, state_size, own_rows).transpose(1, 0, 2)
        write_half = lax.dot_general(
            input_rows, weight_all.reshape(state_size, model), (((1,), (1,)), ((), ())),
            preferred_element_type=f32,
        ).astype(bf16)
        state_local = state_of(write_half, scaled_scan)
        state_before = pl.pallas_call(
            functools.partial(second_kernel, seq_count),
            out_shape=jax.ShapeDtypeStruct((state_size, channels), bf16),
            in_specs=[VMEM] * 2,
            out_specs=VMEM,
            scratch_shapes=exchange + dma(seq_count, seq_count),
            compiler_params=pltpu.CompilerParams(collective_id=1, has_side_effects=True),
            name="forward_states",
        )(state_local, decays)

        kernel_sum = jnp.sum(kernel_mat, axis=0)
        write_grad = jnp.dot(kernel_sum, read_rows.astype(f32), precision=highest)
        write_grad = write_grad + lax.dot_general(
            scaled_scan.astype(bf16), grad_after, (((1,), (1,)), ((), ())), preferred_element_type=f32
        )
        grad_half = write_grad.astype(bf16)
        partial = lax.dot_general(
            grad_half, input_rows, (((0,), (0,)), ((), ())), preferred_element_type=f32
        ).astype(bf16)
        part = partial.reshape(state_size, dp_count, chips, 2, own_rows // seq_count)
        part = part.transpose(3, 2, 1, 0, 4).reshape((2, chips * dp_count) + piece)
        grad_sum = pl.pallas_call(
            functools.partial(third_kernel, seq_count, dp_count),
            out_shape=jax.ShapeDtypeStruct((seq_count,) + piece, bf16),
            in_specs=[VMEM],
            out_specs=VMEM,
            scratch_shapes=[pltpu.VMEM((chips * dp_count,) + piece, bf16)] * 3
            + dma(chips * dp_count, chips * dp_count, seq_count),
            compiler_params=pltpu.CompilerParams(collective_id=2, has_side_effects=True),
            name="reduce_gradient",
        )(part)
        def per_head(a):
            return jnp.sum(a.reshape(a.shape[0], heads, HEAD_DIM), axis=2)

        term_one = decay_total * jnp.sum(
            per_head(grad_after.astype(f32) * state_before.astype(f32)), axis=0)
        grad_write = jnp.dot(write_half, grad_after, preferred_element_type=f32)
        second_rows = to_end * per_head(scan_rows.astype(f32) * grad_write)
        term_two = jnp.cumsum(second_rows, axis=0) - second_rows
        state_read = jnp.dot(read_rows, state_before, preferred_element_type=f32)
        third_rows = from_start * per_head(back_rows.astype(f32) * state_read)
        term_three = jnp.flip(jnp.cumsum(jnp.flip(third_rows, 0), axis=0), 0)
        write_read = jnp.dot(write_half, read_rows.T, preferred_element_type=f32)
        pairing = jnp.where((row_index < col_index)[None], kernel_mat * write_read[None], 0.0)
        balance = (jnp.sum(pairing, axis=2) - jnp.sum(pairing, axis=1)).T
        term_four = jnp.cumsum(balance, axis=0) - balance
        decay_grad = term_one[None, :] + term_two + term_three + term_four
    grad_rows = grad_sum.reshape(seq_count, state_size, own_rows // seq_count).transpose(1, 0, 2)
    grad_rows = grad_rows.reshape(state_size, own_rows).astype(f32).T
    new_weight, new_first, new_second = adam_update(
        grad_rows, write_weight, first_moment, second_moment
    )

    return (decay_grad[None], new_weight, new_first, new_second)


def solution(mesh):
    in_specs = (
        P("dp", "seq", None),
        P("dp", "seq", None),
        P("dp", "seq", None),
        P("dp", "seq", None),
        P("dp", "seq", None),
        P("dp", None),
        P("dp", None),
        P("dp", None),
    )
    out_specs = (P("dp", "seq", None), P("dp", None), P("dp", None), P("dp", None))
    return jax.shard_map(
        on_device, mesh=mesh, in_specs=in_specs, out_specs=out_specs, check_vma=False
    )
```

```python
import functools

import jax
import jax.numpy as jnp
from jax import lax
from jax.experimental import pallas as pl
from jax.experimental.pallas import tpu as pltpu
from jax.sharding import PartitionSpec as P

HEAD_DIM = 64

beta_one = 0.9
beta_two = 0.999
adam_count = 10.0
learn_rate = 0.01
weight_decay = 0.1
epsilon = 1e-08
highest = lax.Precision.HIGHEST
f32 = jnp.float32
bf16 = jnp.bfloat16
MESH = pl.DeviceIdType.MESH
VMEM = pl.BlockSpec(memory_space=pltpu.VMEM)


def remote(src, dst, send_sem, recv_sem, where):
    return pltpu.make_async_remote_copy(
        src_ref=src, dst_ref=dst, send_sem=send_sem, recv_sem=recv_sem, device_id=where,
        device_id_type=MESH,
    )


def loop(low, high, body):
    lax.fori_loop(low, high, lambda i, carry: (body(i), carry)[1], 0)


class Scan:
    def __init__(self, count, me, local, decay, gathered, sent, result, sems):
        self.count, self.me = count, me
        self.local, self.decay, self.gathered, self.sent, self.result = (
            local, decay, gathered, sent, result)
        self.width = local.shape[1] // count
        self.out_send, self.out_recv, self.back_send, self.back_recv = sems

    def columns(self, place):
        return pl.ds(pl.multiple_of(place * self.width, self.width), self.width)

    def outward(self, j, source):
        return remote(self.local.at[:, self.columns(j)], self.gathered.at[source],
                      self.out_send.at[j], self.out_recv.at[source], {"seq": j})

    def homeward(self, i, owner):
        return remote(self.sent.at[i], self.result.at[:, self.columns(owner)],
                      self.back_send.at[i], self.back_recv.at[owner], {"seq": i})

    def start(self):
        loop(1, self.count,
             lambda k: self.outward(lax.rem(self.me + k, self.count), self.me).start())
        self.gathered[self.me] = self.local[:, self.columns(self.me)]

    def combine(self, reverse):
        count, me = self.count, self.me

        def one(k, running):
            i = count - 1 - k if reverse else k

            @pl.when(i != me)
            def _():
                self.outward(i, i).wait_recv()

            self.sent[i] = running.astype(self.sent.dtype)
            new = self.decay[i] * running + self.gathered[i].astype(f32)

            @pl.when(i != me)
            def _():
                self.homeward(i, me).start()

            return new

        lax.fori_loop(0, count, one, jnp.zeros(self.gathered.shape[1:], f32))
        self.result[:, self.columns(me)] = self.sent[me]

    def arrive(self):
        def one(k):
            j = lax.rem(self.me + k, self.count)
            self.homeward(j, j).wait_recv()

        loop(1, self.count, one)

    def drain(self):
        def one(k):
            j = lax.rem(self.me + k, self.count)
            self.outward(j, j).wait_send()
            self.homeward(j, j).wait_send()

        loop(1, self.count, one)

    def finish(self):
        self.arrive()
        self.drain()


def greet(seq_count, dp_count, same_core):
    seq_me, dp_me = lax.axis_index("seq"), lax.axis_index("dp")
    barrier = pltpu.get_barrier_semaphore()
    loop(1, seq_count, lambda k: pl.semaphore_signal(
        barrier, inc=1, device_id={"seq": lax.rem(seq_me + k, seq_count)}, device_id_type=MESH))
    total = seq_count - 1
    places = seq_count // 2 if same_core else 1

    def over(k):
        d = lax.rem(dp_me + 1 + k // places, dp_count)
        s = lax.rem(seq_me + 2 * (k % places), seq_count)
        pl.semaphore_signal(barrier, inc=1, device_id={"seq": s, "dp": d}, device_id_type=MESH)

    loop(0, (dp_count - 1) * places, over)
    return lambda: pl.semaphore_wait(barrier, total + (dp_count - 1) * places)


def first_kernel(seq_count, dp_count, weight, local, decay, weights, decays, result,
                 gathered, sent, w_send, w_recv, p_send, p_recv, d_send, d_recv,
                 a_send, a_recv, b_send, b_recv):
    seq_me, dp_me = lax.axis_index("seq"), lax.axis_index("dp")
    core = lax.rem(seq_me, 2)
    partner = seq_me + 1 - 2 * core
    greet(seq_count, dp_count, False)()

    def across(d, source):
        return remote(weight.at[core], weights.at[source, core], w_send.at[d], w_recv.at[source],
                      {"dp": d})

    def beside(d, half):
        return remote(weights.at[d, half], weights.at[d, half], p_send.at[d], p_recv.at[d],
                      {"seq": partner})

    def tell(j, source):
        return remote(decay.at[j], decays.at[source], d_send.at[j], d_recv.at[source], {"seq": j})

    loop(1, dp_count, lambda k: across(lax.rem(dp_me + k, dp_count), dp_me).start())
    loop(1, seq_count, lambda k: tell(lax.rem(seq_me + k, seq_count), seq_me).start())
    scan = Scan(seq_count, seq_me, local, decays, gathered, sent, result,
                (a_send, a_recv, b_send, b_recv))
    scan.start()
    decays[seq_me] = decay[seq_me]
    weights[dp_me] = weight[...]

    def told(k):
        j = lax.rem(seq_me + k, seq_count)
        tell(j, j).wait_recv()

    loop(1, seq_count, told)

    def pass_on(k):
        d = lax.rem(dp_me + k, dp_count)
        across(d, d).wait_recv()
        beside(d, core).start()

    loop(1, dp_count, pass_on)
    scan.combine(True)

    def end(k):
        d = lax.rem(dp_me + k, dp_count)
        across(d, d).wait_send()
        beside(d, core).wait_send()
        beside(d, 1 - core).wait_recv()

    loop(1, dp_count, end)
    loop(1, seq_count, lambda k: tell(lax.rem(seq_me + k, seq_count), 0).wait_send())
    scan.finish()


def second_kernel(seq_count, local, decays, result, gathered, sent, a_send, a_recv, b_send, b_recv):
    greet(seq_count, 1, False)()
    scan = Scan(seq_count, lax.axis_index("seq"), local, decays, gathered, sent, result,
                (a_send, a_recv, b_send, b_recv))
    scan.start()
    scan.combine(False)
    scan.finish()


def third_kernel(seq_count, dp_count, part, total, halves, summed, pieces,
                 h_send, h_recv, s_send, s_recv, g_send, g_recv):
    seq_me, dp_me = lax.axis_index("seq"), lax.axis_index("dp")
    core = lax.rem(seq_me, 2)
    chip = seq_me // 2
    partner = seq_me + 1 - 2 * core
    group = (seq_count // 2) * dp_count
    mine = chip * dp_count + dp_me
    greet(seq_count, dp_count, True)()

    def half(g):
        return remote(part.at[1 - core, g], halves.at[g], h_send.at[g], h_recv.at[g],
                      {"seq": partner})

    def scatter(g, source):
        return remote(summed.at[g], pieces.at[source], s_send.at[g], s_recv.at[source],
                      {"seq": 2 * (g // dp_count) + core, "dp": g % dp_count})

    def share(j, source):
        return remote(total.at[seq_me], total.at[source], g_send.at[j], g_recv.at[source],
                      {"seq": j})

    loop(1, group + 1, lambda k: half(lax.rem(mine + k, group)).start())

    def pair(k):
        g = lax.rem(mine + k, group)
        half(g).wait_recv()
        summed[g] = (part[core, g].astype(f32) + halves[g].astype(f32)).astype(bf16)

        @pl.when(g != mine)
        def _():
            scatter(g, mine).start()

    loop(1, group + 1, pair)

    def collect(k, running):
        g = lax.rem(mine + group - k, group)
        scatter(g, g).wait_recv()
        return running + pieces[g].astype(f32)

    own = part[core, mine].astype(f32) + halves[mine].astype(f32)
    total[seq_me] = lax.fori_loop(1, group, collect, own).astype(bf16)
    loop(1, seq_count, lambda k: share(lax.rem(seq_me + k, seq_count), seq_me).start())

    def end(k):
        j = lax.rem(seq_me + seq_count - k, seq_count)
        share(j, j).wait_recv()
        share(j, j).wait_send()

    loop(1, group + 1, lambda k: half(lax.rem(mine + k, group)).wait_send())
    loop(1, group, lambda k: scatter(lax.rem(mine + k, group), 0).wait_send())
    loop(1, seq_count, end)


def nt(a, b):
    return lax.dot_general(a, b, (((1,), (1,)), ((), ())), preferred_element_type=f32)


def split(a):
    high = a.astype(bf16)
    return high, (a - high.astype(f32)).astype(bf16)


def exact(a, b):
    return lax.dot_general(a, b, (((1,), (1,)), ((), ())), precision=highest)


def one_kernel(seq_count, dp_count, weight_rows, log_decay, scan_rows, back_rows, read_rows,
               input_rows, decay_grad, total,
               grad_after, state_before, weight, reverse_local, decay, scaled_scan, kernel_mat,
               row_sums, col_sums, weights, decays, forward_local, reverse_got, reverse_sent, forward_got,
               forward_sent, part, halves, summed, pieces,
               w_send, w_recv, p_send, p_recv, d_send, d_recv, a_send, a_recv, b_send, b_recv,
               e_send, e_recv, f_send, f_recv, h_send, h_recv, s_send, s_recv, g_send, g_recv,
               r_send, r_recv):
    seq_me, dp_me = lax.axis_index("seq"), lax.axis_index("dp")
    core = lax.rem(seq_me, 2)
    chip = seq_me // 2
    partner = seq_me + 1 - 2 * core
    group = (seq_count // 2) * dp_count
    mine = chip * dp_count + dp_me
    ready = greet(seq_count, dp_count, True)
    length, channels = scan_rows.shape
    heads = channels // HEAD_DIM
    state_size = read_rows.shape[0]
    row_index = lax.broadcasted_iota(jnp.int32, (length, length), 0)
    col_index = lax.broadcasted_iota(jnp.int32, (length, length), 1)
    causal = row_index <= col_index
    before = (col_index < row_index).astype(f32)
    upto = (col_index <= row_index).astype(f32)
    onward = causal.astype(f32)
    run_cols = exact(upto, log_decay[...])
    run_rows = exact(log_decay[...], upto)
    overall = run_cols[length - 1 :, :]
    to_end = jnp.exp(overall - run_cols)
    from_start = jnp.exp(run_cols)
    owner = lax.broadcasted_iota(jnp.int32, (heads, channels), 0)
    spot = lax.broadcasted_iota(jnp.int32, (heads, channels), 1) - owner * HEAD_DIM
    member = ((spot >= 0) & (spot < HEAD_DIM)).astype(bf16)

    def widen(a):
        high, low = split(a)
        return (jnp.dot(high, member, preferred_element_type=f32)
                + jnp.dot(low, member, preferred_element_type=f32))

    def per_head(a):
        high, low = split(a)
        return nt(high, member) + nt(low, member)

    back_high, back_low = split(back_rows[...].astype(f32) * widen(from_start))
    reverse_local[...] = (
        jnp.dot(read_rows[...], back_high, preferred_element_type=f32)
        + jnp.dot(read_rows[...], back_low, preferred_element_type=f32)
    ).astype(bf16)
    decay_wide = widen(jnp.exp(jnp.broadcast_to(overall, (8, heads))))[:1]
    width = channels // seq_count
    for j in range(seq_count):
        decay[j] = decay_wide[:, j * width : (j + 1) * width]
    for side in range(2):
        weight[side] = weight_rows[
            side * state_size // 2 : (side + 1) * state_size // 2, :].astype(bf16)
    ready()

    def across(d, source):
        return remote(weight.at[core], weights.at[source, core], w_send.at[d], w_recv.at[source],
                      {"dp": d})

    def beside(d, half):
        return remote(weights.at[d, half], weights.at[d, half], p_send.at[d], p_recv.at[d],
                      {"seq": partner})

    def tell(j, source):
        return remote(decay.at[j], decays.at[source], d_send.at[j], d_recv.at[source], {"seq": j})

    def half(g):
        return remote(part.at[1 - core, g], halves.at[g], h_send.at[g], h_recv.at[g],
                      {"seq": partner})

    def scatter(g, source):
        return remote(summed.at[g], pieces.at[source], s_send.at[g], s_recv.at[source],
                      {"seq": 2 * (g // dp_count) + core, "dp": g % dp_count})

    def share(j, source):
        return remote(total.at[seq_me], total.at[source], g_send.at[j], g_recv.at[source],
                      {"seq": j})

    def relay(j, source):
        return remote(total.at[j], total.at[source], r_send.at[j], r_recv.at[source],
                      {"seq": partner})

    def fellow(k):
        return lax.rem(seq_me + 2 * k, seq_count)

    loop(1, dp_count, lambda k: across(lax.rem(dp_me + k, dp_count), dp_me).start())
    loop(1, seq_count, lambda k: tell(lax.rem(seq_me + k, seq_count), seq_me).start())
    reverse = Scan(seq_count, seq_me, reverse_local, decays, reverse_got, reverse_sent, grad_after,
                   (a_send, a_recv, b_send, b_recv))
    forward = Scan(seq_count, seq_me, forward_local, decays, forward_got, forward_sent,
                   state_before, (e_send, e_recv, f_send, f_recv))
    reverse.start()
    decays[seq_me] = decay[seq_me]
    weights[dp_me] = weight[...]

    kernel_sum = jnp.zeros((length, length), f32)
    scaled_scan[...] = scan_rows[...].astype(f32) * widen(to_end)
    for h in range(heads):
        at = slice(h * HEAD_DIM, (h + 1) * HEAD_DIM)
        crossed = nt(scan_rows[:, at], back_rows[:, at])
        spread = run_rows[h : h + 1, :] - run_cols[:, h : h + 1]
        term = jnp.where(causal, jnp.exp(jnp.minimum(spread, 0.0)), 0.0) * crossed
        kernel_mat[h] = term
        kernel_sum += term

    def pass_on(k):
        d = lax.rem(dp_me + k, dp_count)
        across(d, d).wait_recv()
        beside(d, core).start()

    def told(k):
        j = lax.rem(seq_me + k, seq_count)
        tell(j, j).wait_recv()

    loop(1, dp_count, pass_on)
    loop(1, seq_count, told)
    reverse.combine(True)

    def beside_end(k):
        d = lax.rem(dp_me + k, dp_count)
        beside(d, 1 - core).wait_recv()

    loop(1, dp_count, beside_end)
    own_rows = weight.shape[2]
    write = []
    for side in range(2):
        some = nt(weights[0, side], input_rows[:, :own_rows])
        for d in range(1, dp_count):
            some += nt(weights[d, side], input_rows[:, d * own_rows : (d + 1) * own_rows])
        write.append(some)
    write = jnp.concatenate(write, axis=0)
    write_rows = write.T.astype(bf16)
    write = write.astype(bf16)
    step = channels // 4
    for low in range(0, channels, step):
        scan_high, scan_low = split(scaled_scan[:, low : low + step])
        forward_local[:, low : low + step] = (
            jnp.dot(write, scan_high, preferred_element_type=f32)
            + jnp.dot(write, scan_low, preferred_element_type=f32)
        )
    forward.start()

    reverse.arrive()
    sum_high, sum_low = split(kernel_sum)
    write_grad = nt(grad_after[...], scaled_scan[...].astype(bf16))
    write_grad += nt(read_rows[...], sum_high) + nt(read_rows[...], sum_low)
    grad_half = write_grad.astype(bf16)
    wide = own_rows // seq_count
    for g in range(group):
        low = (g % dp_count) * own_rows + 2 * (g // dp_count) * wide
        term = jnp.dot(grad_half, input_rows[:, low : low + 2 * wide],
                       preferred_element_type=f32).astype(bf16)
        part[0, g] = term[:, :wide]
        part[1, g] = term[:, wide:]
    loop(1, group + 1, lambda k: half(lax.rem(mine + k, group)).start())
    def pair(k):
        g = lax.rem(mine + k, group)
        half(g).wait_recv()
        summed[g] = (part[core, g].astype(f32) + halves[g].astype(f32)).astype(bf16)

        @pl.when(g != mine)
        def _():
            scatter(g, mine).start()

    loop(1, group + 1, pair)
    forward.combine(False)

    read_turned = read_rows[...].astype(f32).T.astype(bf16)
    write_read = jnp.where(row_index < col_index, nt(write_rows, read_turned), 0.0)
    for h in range(heads):
        pairing = kernel_mat[h] * write_read
        row_sums[:, h : h + 1] = jnp.sum(pairing, axis=1, keepdims=True)
        col_sums[h : h + 1, :] = jnp.sum(pairing, axis=0, keepdims=True)
    grad_write = jnp.dot(write_rows, grad_after[...], preferred_element_type=f32)
    second = to_end * per_head(scan_rows[...].astype(f32) * grad_write) + row_sums[...]

    def collect(k, running):
        g = lax.rem(mine + group - k, group)
        scatter(g, g).wait_recv()
        return running + pieces[g].astype(f32)

    own = part[core, mine].astype(f32) + halves[mine].astype(f32)
    total[seq_me] = lax.fori_loop(1, group, collect, own).astype(bf16)
    loop(1, seq_count // 2, lambda k: share(fellow(k), seq_me).start())
    relay(seq_me, seq_me).start()
    forward.arrive()
    state_high, state_low = split(state_before[...])
    state_read = (jnp.dot(read_turned, state_high, preferred_element_type=f32)
                  + jnp.dot(read_turned, state_low, preferred_element_type=f32))
    third = from_start * per_head(back_rows[...].astype(f32) * state_read)
    both = jnp.sum(grad_after[...].astype(f32) * state_before[...], axis=0,
                   keepdims=True)
    first = jnp.exp(overall) * per_head(jnp.broadcast_to(both, (8, channels)))[:1]
    decay_grad[...] = jnp.transpose(
        first
        + jnp.dot(before, second, precision=highest)
        - exact(before, col_sums[...])
        + jnp.dot(onward, third, precision=highest)
    )

    def shared(k):
        j = fellow(seq_count // 2 - k)
        share(j, j).wait_recv()
        relay(j, j).start()

    loop(1, seq_count // 2, shared)

    def end(k):
        share(fellow(k), seq_me).wait_send()

    def relayed(k):
        j = fellow(k)
        relay(j, j).wait_send()
        other = j + 1 - 2 * core
        relay(other, other).wait_recv()

    def dp_end(k):
        d = lax.rem(dp_me + k, dp_count)
        across(d, d).wait_send()
        beside(d, core).wait_send()

    loop(1, dp_count, dp_end)
    reverse.drain()
    forward.drain()
    loop(1, group + 1, lambda k: half(lax.rem(mine + k, group)).wait_send())
    loop(1, group, lambda k: scatter(lax.rem(mine + k, group), 0).wait_send())
    loop(1, seq_count, lambda k: tell(lax.rem(seq_me + k, seq_count), seq_me).wait_send())
    loop(1, seq_count // 2, end)
    loop(0, seq_count // 2, relayed)


def dma(*sizes):
    return [pltpu.SemaphoreType.DMA((size,)) for size in sizes for _ in range(2)]


def adam_update(grad_rows, weight_rows, first_rows, second_rows):
    new_first = beta_one * first_rows + (1.0 - beta_one) * grad_rows
    new_second = beta_two * second_rows + (1.0 - beta_two) * grad_rows * grad_rows
    first_hat = new_first / (1.0 - beta_one**adam_count)
    second_hat = new_second / (1.0 - beta_two**adam_count)
    new_weight = weight_rows - learn_rate * (
        first_hat / (jnp.sqrt(second_hat) + epsilon) + weight_decay * weight_rows
    )
    return (new_weight, new_first, new_second)


def on_device(
    layer_input,
    scan_input,
    readout,
    log_decay,
    output_cotangent,
    write_weight,
    first_moment,
    second_moment,
):
    seq_count, dp_count = lax.axis_size("seq"), lax.axis_size("dp")
    input_rows = layer_input[0]
    scan_rows = scan_input[0]
    read_rows = readout[0]
    decay_rows = log_decay[0]
    back_rows = output_cotangent[0]
    length, model = input_rows.shape
    heads = decay_rows.shape[1]
    channels = scan_rows.shape[1]
    state_size = read_rows.shape[1]
    own_rows = write_weight.shape[0]
    width = channels // seq_count

    chips = seq_count // 2
    group = chips * dp_count
    if own_rows % (128 * seq_count) == 0:
        piece = (state_size, own_rows // seq_count)
        exchange = [pltpu.VMEM((seq_count, state_size, width), bf16)] * 2
        exact_exchange = [pltpu.VMEM((seq_count, state_size, width), f32)] * 2
        states = pltpu.VMEM((state_size, channels), bf16)
        exact_states = pltpu.VMEM((state_size, channels), f32)
        halves = (2, state_size // 2, own_rows)
        decay_grad, grad_sum = pl.pallas_call(
            functools.partial(one_kernel, seq_count, dp_count),
            out_shape=(
                jax.ShapeDtypeStruct((heads, length), f32),
                jax.ShapeDtypeStruct((seq_count,) + piece, bf16),
            ),
            in_specs=[VMEM] * 6,
            out_specs=[VMEM] * 2,
            scratch_shapes=[
                states,
                exact_states,
                pltpu.VMEM(halves, bf16),
                states,
                pltpu.VMEM((seq_count, 1, width), f32),
                pltpu.VMEM((length, channels), f32),
                pltpu.VMEM((heads, length, length), f32),
                pltpu.VMEM((length, heads), f32),
                pltpu.VMEM((heads, length), f32),
                pltpu.VMEM((dp_count,) + halves, bf16),
                pltpu.VMEM((seq_count, 1, width), f32),
                exact_states,
            ]
            + exchange
            + exact_exchange
            + [pltpu.VMEM((2, group) + piece, bf16)]
            + [pltpu.VMEM((group,) + piece, bf16)] * 3
            + dma(dp_count, dp_count, seq_count, seq_count, seq_count, seq_count, seq_count,
                  group, group, seq_count, seq_count),
            compiler_params=pltpu.CompilerParams(collective_id=3, has_side_effects=True),
            name="whole_step",
        )(write_weight.T, decay_rows.T, scan_rows, back_rows, read_rows.T, input_rows)
        decay_grad = decay_grad.T
    else:
        running = jnp.cumsum(decay_rows, axis=0)
        overall = running[-1]
        to_end = jnp.exp(overall[None, :] - running)
        from_start = jnp.exp(running)
        decay_total = jnp.exp(overall)

        def widen(a):
            return jnp.repeat(a, HEAD_DIM, axis=1)

        scaled_scan = scan_rows.astype(f32) * widen(to_end)
        scaled_back = back_rows.astype(f32) * widen(from_start)

        def state_of(vectors, rows):
            return lax.dot_general(
                vectors.astype(f32), rows, (((0,), (0,)), ((), ())), precision=highest
            )

        reverse_local = state_of(read_rows, scaled_back).astype(bf16)
        decay_lanes = widen(decay_total[None]).reshape(seq_count, 1, width)
        weight_half = write_weight.T.astype(bf16).reshape(2, state_size // 2, own_rows)
        exchange = [
            pltpu.VMEM((seq_count, state_size, width), bf16),
            pltpu.VMEM((seq_count, state_size, width), bf16),
        ]
        piece = (state_size * own_rows // seq_count // 128, 128)
        scan_split = scan_rows.reshape(length, heads, HEAD_DIM)
        back_split = back_rows.reshape(length, heads, HEAD_DIM)
        crossed = jnp.einsum("thp,shp->hts", scan_split, back_split, preferred_element_type=f32)
        heads_running = running.T
        spread = heads_running[:, None, :] - heads_running[:, :, None]
        row_index = lax.broadcasted_iota(jnp.int32, (length, length), 0)
        col_index = lax.broadcasted_iota(jnp.int32, (length, length), 1)
        kernel_mat = (
            jnp.where((row_index <= col_index)[None], jnp.exp(jnp.minimum(spread, 0.0)), 0.0) * crossed
        )
        weights, decays, grad_after = pl.pallas_call(
            functools.partial(first_kernel, seq_count, dp_count),
            out_shape=(
                jax.ShapeDtypeStruct((dp_count,) + weight_half.shape, bf16),
                jax.ShapeDtypeStruct(decay_lanes.shape, f32),
                jax.ShapeDtypeStruct((state_size, channels), bf16),
            ),
            in_specs=[VMEM] * 3,
            out_specs=[VMEM] * 3,
            scratch_shapes=exchange + dma(dp_count, dp_count, seq_count, seq_count, seq_count),
            compiler_params=pltpu.CompilerParams(collective_id=0, has_side_effects=True),
            name="gather_reverse",
        )(weight_half, reverse_local, decay_lanes)

        weight_all = weights.reshape(dp_count, state_size, own_rows).transpose(1, 0, 2)
        write_half = lax.dot_general(
            input_rows, weight_all.reshape(state_size, model), (((1,), (1,)), ((), ())),
            preferred_element_type=f32,
        ).astype(bf16)
        state_local = state_of(write_half, scaled_scan)
        state_before = pl.pallas_call(
            functools.partial(second_kernel, seq_count),
            out_shape=jax.ShapeDtypeStruct((state_size, channels), f32),
            in_specs=[VMEM] * 2,
            out_specs=VMEM,
            scratch_shapes=[pltpu.VMEM((seq_count, state_size, width), f32)] * 2 + dma(seq_count, seq_count),
            compiler_params=pltpu.CompilerParams(collective_id=1, has_side_effects=True),
            name="forward_states",
        )(state_local, decays)

        kernel_sum = jnp.sum(kernel_mat, axis=0)
        write_grad = jnp.dot(kernel_sum, read_rows.astype(f32), precision=highest)
        write_grad = write_grad + lax.dot_general(
            scaled_scan.astype(bf16), grad_after, (((1,), (1,)), ((), ())), preferred_element_type=f32
        )
        grad_half = write_grad.astype(bf16)
        partial = lax.dot_general(
            grad_half, input_rows, (((0,), (0,)), ((), ())), preferred_element_type=f32
        ).astype(bf16)
        part = partial.reshape(state_size, dp_count, chips, 2, own_rows // seq_count)
        part = part.transpose(3, 2, 1, 0, 4).reshape((2, chips * dp_count) + piece)
        grad_sum = pl.pallas_call(
            functools.partial(third_kernel, seq_count, dp_count),
            out_shape=jax.ShapeDtypeStruct((seq_count,) + piece, bf16),
            in_specs=[VMEM],
            out_specs=VMEM,
            scratch_shapes=[pltpu.VMEM((chips * dp_count,) + piece, bf16)] * 3
            + dma(chips * dp_count, chips * dp_count, seq_count),
            compiler_params=pltpu.CompilerParams(collective_id=2, has_side_effects=True),
            name="reduce_gradient",
        )(part)
        def per_head(a):
            return jnp.sum(a.reshape(a.shape[0], heads, HEAD_DIM), axis=2)

        term_one = decay_total * jnp.sum(
            per_head(grad_after.astype(f32) * state_before.astype(f32)), axis=0)
        grad_write = jnp.dot(write_half, grad_after, preferred_element_type=f32)
        second_rows = to_end * per_head(scan_rows.astype(f32) * grad_write)
        term_two = jnp.cumsum(second_rows, axis=0) - second_rows
        state_read = jnp.dot(read_rows.astype(f32), state_before, precision=highest)
        third_rows = from_start * per_head(back_rows.astype(f32) * state_read)
        term_three = jnp.flip(jnp.cumsum(jnp.flip(third_rows, 0), axis=0), 0)
        write_read = jnp.dot(write_half, read_rows.T, preferred_element_type=f32)
        pairing = jnp.where((row_index < col_index)[None], kernel_mat * write_read[None], 0.0)
        balance = (jnp.sum(pairing, axis=2) - jnp.sum(pairing, axis=1)).T
        term_four = jnp.cumsum(balance, axis=0) - balance
        decay_grad = term_one[None, :] + term_two + term_three + term_four
    grad_rows = grad_sum.reshape(seq_count, state_size, own_rows // seq_count).transpose(1, 0, 2)
    grad_rows = grad_rows.reshape(state_size, own_rows).astype(f32).T
    new_weight, new_first, new_second = adam_update(
        grad_rows, write_weight, first_moment, second_moment
    )

    return (decay_grad[None], new_weight, new_first, new_second)


def solution(mesh):
    in_specs = (
        P("dp", "seq", None),
        P("dp", "seq", None),
        P("dp", "seq", None),
        P("dp", "seq", None),
        P("dp", "seq", None),
        P("dp", None),
        P("dp", None),
        P("dp", None),
    )
    out_specs = (P("dp", "seq", None), P("dp", None), P("dp", None), P("dp", None))
    return jax.shard_map(
        on_device, mesh=mesh, in_specs=in_specs, out_specs=out_specs, check_vma=False
    )
```

```python
import functools

import jax
import jax.numpy as jnp
from jax import lax
from jax.experimental import pallas as pl
from jax.experimental.pallas import tpu as pltpu
from jax.sharding import PartitionSpec as P

HEAD_DIM = 64

beta_one = 0.9
beta_two = 0.999
adam_count = 10.0
learn_rate = 0.01
weight_decay = 0.1
epsilon = 1e-08
highest = lax.Precision.HIGHEST
f32 = jnp.float32
bf16 = jnp.bfloat16
MESH = pl.DeviceIdType.MESH
VMEM = pl.BlockSpec(memory_space=pltpu.VMEM)


def remote(src, dst, send_sem, recv_sem, where):
    return pltpu.make_async_remote_copy(
        src_ref=src, dst_ref=dst, send_sem=send_sem, recv_sem=recv_sem, device_id=where,
        device_id_type=MESH,
    )


def loop(low, high, body):
    lax.fori_loop(low, high, lambda i, carry: (body(i), carry)[1], 0)


class Scan:
    def __init__(self, count, me, local, decay, gathered, sent, result, sems):
        self.count, self.me = count, me
        self.local, self.decay, self.gathered, self.sent, self.result = (
            local, decay, gathered, sent, result)
        self.width = local.shape[1] // count
        self.out_send, self.out_recv, self.back_send, self.back_recv = sems

    def columns(self, place):
        return pl.ds(pl.multiple_of(place * self.width, self.width), self.width)

    def outward(self, j, source):
        return remote(self.local.at[:, self.columns(j)], self.gathered.at[source],
                      self.out_send.at[j], self.out_recv.at[source], {"seq": j})

    def homeward(self, i, owner):
        return remote(self.sent.at[i], self.result.at[:, self.columns(owner)],
                      self.back_send.at[i], self.back_recv.at[owner], {"seq": i})

    def start(self):
        loop(1, self.count,
             lambda k: self.outward(lax.rem(self.me + k, self.count), self.me).start())
        self.gathered[self.me] = self.local[:, self.columns(self.me)]

    def combine(self, reverse):
        count, me = self.count, self.me

        def one(k, running):
            i = count - 1 - k if reverse else k

            @pl.when(i != me)
            def _():
                self.outward(i, i).wait_recv()

            self.sent[i] = running.astype(self.sent.dtype)
            new = self.decay[i] * running + self.gathered[i].astype(f32)

            @pl.when(i != me)
            def _():
                self.homeward(i, me).start()

            return new

        lax.fori_loop(0, count, one, jnp.zeros(self.gathered.shape[1:], f32))
        self.result[:, self.columns(me)] = self.sent[me]

    def arrive(self):
        def one(k):
            j = lax.rem(self.me + k, self.count)
            self.homeward(j, j).wait_recv()

        loop(1, self.count, one)

    def drain(self):
        def one(k):
            j = lax.rem(self.me + k, self.count)
            self.outward(j, j).wait_send()
            self.homeward(j, j).wait_send()

        loop(1, self.count, one)

    def finish(self):
        self.arrive()
        self.drain()


def greet(seq_count, dp_count, same_core):
    seq_me, dp_me = lax.axis_index("seq"), lax.axis_index("dp")
    barrier = pltpu.get_barrier_semaphore()
    loop(1, seq_count, lambda k: pl.semaphore_signal(
        barrier, inc=1, device_id={"seq": lax.rem(seq_me + k, seq_count)}, device_id_type=MESH))
    total = seq_count - 1
    places = seq_count // 2 if same_core else 1

    def over(k):
        d = lax.rem(dp_me + 1 + k // places, dp_count)
        s = lax.rem(seq_me + 2 * (k % places), seq_count)
        pl.semaphore_signal(barrier, inc=1, device_id={"seq": s, "dp": d}, device_id_type=MESH)

    loop(0, (dp_count - 1) * places, over)
    return lambda: pl.semaphore_wait(barrier, total + (dp_count - 1) * places)


def first_kernel(seq_count, dp_count, weight, local, decay, weights, decays, result,
                 gathered, sent, w_send, w_recv, p_send, p_recv, d_send, d_recv,
                 a_send, a_recv, b_send, b_recv):
    seq_me, dp_me = lax.axis_index("seq"), lax.axis_index("dp")
    core = lax.rem(seq_me, 2)
    partner = seq_me + 1 - 2 * core
    greet(seq_count, dp_count, False)()

    def across(d, source):
        return remote(weight.at[core], weights.at[source, core], w_send.at[d], w_recv.at[source],
                      {"dp": d})

    def beside(d, half):
        return remote(weights.at[d, half], weights.at[d, half], p_send.at[d], p_recv.at[d],
                      {"seq": partner})

    def tell(j, source):
        return remote(decay.at[j], decays.at[source], d_send.at[j], d_recv.at[source], {"seq": j})

    loop(1, dp_count, lambda k: across(lax.rem(dp_me + k, dp_count), dp_me).start())
    loop(1, seq_count, lambda k: tell(lax.rem(seq_me + k, seq_count), seq_me).start())
    scan = Scan(seq_count, seq_me, local, decays, gathered, sent, result,
                (a_send, a_recv, b_send, b_recv))
    scan.start()
    decays[seq_me] = decay[seq_me]
    weights[dp_me] = weight[...]

    def told(k):
        j = lax.rem(seq_me + k, seq_count)
        tell(j, j).wait_recv()

    loop(1, seq_count, told)

    def pass_on(k):
        d = lax.rem(dp_me + k, dp_count)
        across(d, d).wait_recv()
        beside(d, core).start()

    loop(1, dp_count, pass_on)
    scan.combine(True)

    def end(k):
        d = lax.rem(dp_me + k, dp_count)
        across(d, d).wait_send()
        beside(d, core).wait_send()
        beside(d, 1 - core).wait_recv()

    loop(1, dp_count, end)
    loop(1, seq_count, lambda k: tell(lax.rem(seq_me + k, seq_count), 0).wait_send())
    scan.finish()


def second_kernel(seq_count, local, decays, result, gathered, sent, a_send, a_recv, b_send, b_recv):
    greet(seq_count, 1, False)()
    scan = Scan(seq_count, lax.axis_index("seq"), local, decays, gathered, sent, result,
                (a_send, a_recv, b_send, b_recv))
    scan.start()
    scan.combine(False)
    scan.finish()


def third_kernel(seq_count, dp_count, part, total, halves, summed, pieces,
                 h_send, h_recv, s_send, s_recv, g_send, g_recv):
    seq_me, dp_me = lax.axis_index("seq"), lax.axis_index("dp")
    core = lax.rem(seq_me, 2)
    chip = seq_me // 2
    partner = seq_me + 1 - 2 * core
    group = (seq_count // 2) * dp_count
    mine = chip * dp_count + dp_me
    greet(seq_count, dp_count, True)()

    def half(g):
        return remote(part.at[1 - core, g], halves.at[g], h_send.at[g], h_recv.at[g],
                      {"seq": partner})

    def scatter(g, source):
        return remote(summed.at[g], pieces.at[source], s_send.at[g], s_recv.at[source],
                      {"seq": 2 * (g // dp_count) + core, "dp": g % dp_count})

    def share(j, source):
        return remote(total.at[seq_me], total.at[source], g_send.at[j], g_recv.at[source],
                      {"seq": j})

    loop(1, group + 1, lambda k: half(lax.rem(mine + k, group)).start())

    def pair(k):
        g = lax.rem(mine + k, group)
        half(g).wait_recv()
        summed[g] = (part[core, g].astype(f32) + halves[g].astype(f32)).astype(bf16)

        @pl.when(g != mine)
        def _():
            scatter(g, mine).start()

    loop(1, group + 1, pair)

    def collect(k, running):
        g = lax.rem(mine + group - k, group)
        scatter(g, g).wait_recv()
        return running + pieces[g].astype(f32)

    own = part[core, mine].astype(f32) + halves[mine].astype(f32)
    total[seq_me] = lax.fori_loop(1, group, collect, own).astype(bf16)
    loop(1, seq_count, lambda k: share(lax.rem(seq_me + k, seq_count), seq_me).start())

    def end(k):
        j = lax.rem(seq_me + seq_count - k, seq_count)
        share(j, j).wait_recv()
        share(j, j).wait_send()

    loop(1, group + 1, lambda k: half(lax.rem(mine + k, group)).wait_send())
    loop(1, group, lambda k: scatter(lax.rem(mine + k, group), 0).wait_send())
    loop(1, seq_count, end)


def nt(a, b):
    return lax.dot_general(a, b, (((1,), (1,)), ((), ())), preferred_element_type=f32)


def split(a):
    high = a.astype(bf16)
    return high, (a - high.astype(f32)).astype(bf16)


def exact(a, b):
    return lax.dot_general(a, b, (((1,), (1,)), ((), ())), precision=highest)


def one_kernel(seq_count, dp_count, weight_rows, log_decay, scan_rows, back_rows, read_rows,
               input_rows, decay_grad, total,
               grad_after, state_before, weight, reverse_local, decay, scaled_scan, kernel_mat,
               row_sums, col_sums, weights, decays, forward_local, reverse_got, reverse_sent, forward_got,
               forward_sent, part, halves, summed, pieces,
               w_send, w_recv, p_send, p_recv, d_send, d_recv, a_send, a_recv, b_send, b_recv,
               e_send, e_recv, f_send, f_recv, h_send, h_recv, s_send, s_recv, g_send, g_recv,
               r_send, r_recv):
    seq_me, dp_me = lax.axis_index("seq"), lax.axis_index("dp")
    core = lax.rem(seq_me, 2)
    chip = seq_me // 2
    partner = seq_me + 1 - 2 * core
    group = (seq_count // 2) * dp_count
    mine = chip * dp_count + dp_me
    ready = greet(seq_count, dp_count, True)
    length, channels = scan_rows.shape
    heads = channels // HEAD_DIM
    state_size = read_rows.shape[0]
    row_index = lax.broadcasted_iota(jnp.int32, (length, length), 0)
    col_index = lax.broadcasted_iota(jnp.int32, (length, length), 1)
    causal = row_index <= col_index
    before = (col_index < row_index).astype(f32)
    upto = (col_index <= row_index).astype(f32)
    onward = causal.astype(f32)
    run_cols = exact(upto, log_decay[...])
    run_rows = exact(log_decay[...], upto)
    overall = run_cols[length - 1 :, :]
    to_end = jnp.exp(overall - run_cols)
    from_start = jnp.exp(run_cols)
    owner = lax.broadcasted_iota(jnp.int32, (heads, channels), 0)
    spot = lax.broadcasted_iota(jnp.int32, (heads, channels), 1) - owner * HEAD_DIM
    member = ((spot >= 0) & (spot < HEAD_DIM)).astype(bf16)

    def widen(a):
        high, low = split(a)
        return (jnp.dot(high, member, preferred_element_type=f32)
                + jnp.dot(low, member, preferred_element_type=f32))

    def per_head(a):
        high, low = split(a)
        return nt(high, member) + nt(low, member)

    back_high, back_low = split(back_rows[...].astype(f32) * widen(from_start))
    reverse_local[...] = (
        jnp.dot(read_rows[...], back_high, preferred_element_type=f32)
        + jnp.dot(read_rows[...], back_low, preferred_element_type=f32)
    ).astype(bf16)
    decay_wide = widen(jnp.exp(jnp.broadcast_to(overall, (8, heads))))[:1]
    width = channels // seq_count
    for j in range(seq_count):
        decay[j] = decay_wide[:, j * width : (j + 1) * width]
    for side in range(2):
        weight[side] = weight_rows[
            side * state_size // 2 : (side + 1) * state_size // 2, :].astype(bf16)
    ready()

    def across(d, source):
        return remote(weight.at[core], weights.at[source, core], w_send.at[d], w_recv.at[source],
                      {"dp": d})

    def beside(d, half):
        return remote(weights.at[d, half], weights.at[d, half], p_send.at[d], p_recv.at[d],
                      {"seq": partner})

    def tell(j, source):
        return remote(decay.at[j], decays.at[source], d_send.at[j], d_recv.at[source], {"seq": j})

    def half(g):
        return remote(part.at[1 - core, g], halves.at[g], h_send.at[g], h_recv.at[g],
                      {"seq": partner})

    def scatter(g, source):
        return remote(summed.at[g], pieces.at[source], s_send.at[g], s_recv.at[source],
                      {"seq": 2 * (g // dp_count) + core, "dp": g % dp_count})

    def share(j, source):
        return remote(total.at[seq_me], total.at[source], g_send.at[j], g_recv.at[source],
                      {"seq": j})

    def relay(j, source):
        return remote(total.at[j], total.at[source], r_send.at[j], r_recv.at[source],
                      {"seq": partner})

    def fellow(k):
        return lax.rem(seq_me + 2 * k, seq_count)

    loop(1, dp_count, lambda k: across(lax.rem(dp_me + k, dp_count), dp_me).start())
    loop(1, seq_count, lambda k: tell(lax.rem(seq_me + k, seq_count), seq_me).start())
    reverse = Scan(seq_count, seq_me, reverse_local, decays, reverse_got, reverse_sent, grad_after,
                   (a_send, a_recv, b_send, b_recv))
    forward = Scan(seq_count, seq_me, forward_local, decays, forward_got, forward_sent,
                   state_before, (e_send, e_recv, f_send, f_recv))
    reverse.start()
    decays[seq_me] = decay[seq_me]
    weights[dp_me] = weight[...]

    kernel_sum = jnp.zeros((length, length), f32)
    scaled_scan[...] = scan_rows[...].astype(f32) * widen(to_end)
    for h in range(heads):
        at = slice(h * HEAD_DIM, (h + 1) * HEAD_DIM)
        crossed = nt(scan_rows[:, at], back_rows[:, at])
        spread = run_rows[h : h + 1, :] - run_cols[:, h : h + 1]
        term = jnp.where(causal, jnp.exp(jnp.minimum(spread, 0.0)), 0.0) * crossed
        kernel_mat[h] = term
        kernel_sum += term

    def pass_on(k):
        d = lax.rem(dp_me + k, dp_count)
        across(d, d).wait_recv()
        beside(d, core).start()

    def told(k):
        j = lax.rem(seq_me + k, seq_count)
        tell(j, j).wait_recv()

    loop(1, dp_count, pass_on)
    loop(1, seq_count, told)
    reverse.combine(True)

    def beside_end(k):
        d = lax.rem(dp_me + k, dp_count)
        beside(d, 1 - core).wait_recv()

    loop(1, dp_count, beside_end)
    own_rows = weight.shape[2]
    write = []
    for side in range(2):
        some = nt(weights[0, side], input_rows[:, :own_rows])
        for d in range(1, dp_count):
            some += nt(weights[d, side], input_rows[:, d * own_rows : (d + 1) * own_rows])
        write.append(some)
    write = jnp.concatenate(write, axis=0)
    write_rows = write.T.astype(bf16)
    write = write.astype(bf16)
    step = channels // 4
    for low in range(0, channels, step):
        scan_high, scan_low = split(scaled_scan[:, low : low + step])
        forward_local[:, low : low + step] = (
            jnp.dot(write, scan_high, preferred_element_type=f32)
            + jnp.dot(write, scan_low, preferred_element_type=f32)
        ).astype(bf16)
    forward.start()

    reverse.arrive()
    sum_high, sum_low = split(kernel_sum)
    write_grad = nt(grad_after[...], scaled_scan[...].astype(bf16))
    write_grad += nt(read_rows[...], sum_high) + nt(read_rows[...], sum_low)
    grad_half = write_grad.astype(bf16)
    wide = own_rows // seq_count
    for g in range(group):
        low = (g % dp_count) * own_rows + 2 * (g // dp_count) * wide
        term = jnp.dot(grad_half, input_rows[:, low : low + 2 * wide],
                       preferred_element_type=f32).astype(bf16)
        part[0, g] = term[:, :wide]
        part[1, g] = term[:, wide:]
    loop(1, group + 1, lambda k: half(lax.rem(mine + k, group)).start())
    def pair(k):
        g = lax.rem(mine + k, group)
        half(g).wait_recv()
        summed[g] = (part[core, g].astype(f32) + halves[g].astype(f32)).astype(bf16)

        @pl.when(g != mine)
        def _():
            scatter(g, mine).start()

    loop(1, group + 1, pair)
    forward.combine(False)

    read_turned = read_rows[...].astype(f32).T.astype(bf16)
    write_read = jnp.where(row_index < col_index, nt(write_rows, read_turned), 0.0)
    for h in range(heads):
        pairing = kernel_mat[h] * write_read
        row_sums[:, h : h + 1] = jnp.sum(pairing, axis=1, keepdims=True)
        col_sums[h : h + 1, :] = jnp.sum(pairing, axis=0, keepdims=True)
    grad_write = jnp.dot(write_rows, grad_after[...], preferred_element_type=f32)
    second = to_end * per_head(scan_rows[...].astype(f32) * grad_write) + row_sums[...]

    def collect(k, running):
        g = lax.rem(mine + group - k, group)
        scatter(g, g).wait_recv()
        return running + pieces[g].astype(f32)

    own = part[core, mine].astype(f32) + halves[mine].astype(f32)
    total[seq_me] = lax.fori_loop(1, group, collect, own).astype(bf16)
    loop(1, seq_count // 2, lambda k: share(fellow(k), seq_me).start())
    relay(seq_me, seq_me).start()
    forward.arrive()
    state_high, state_low = split(state_before[...])
    state_read = (jnp.dot(read_turned, state_high, preferred_element_type=f32)
                  + jnp.dot(read_turned, state_low, preferred_element_type=f32))
    third = from_start * per_head(back_rows[...].astype(f32) * state_read)
    both = jnp.sum(grad_after[...].astype(f32) * state_before[...], axis=0,
                   keepdims=True)
    first = jnp.exp(overall) * per_head(jnp.broadcast_to(both, (8, channels)))[:1]
    decay_grad[...] = jnp.transpose(
        first
        + jnp.dot(before, second, precision=highest)
        - exact(before, col_sums[...])
        + jnp.dot(onward, third, precision=highest)
    )

    def shared(k):
        j = fellow(seq_count // 2 - k)
        share(j, j).wait_recv()
        relay(j, j).start()

    loop(1, seq_count // 2, shared)

    def end(k):
        share(fellow(k), seq_me).wait_send()

    def relayed(k):
        j = fellow(k)
        relay(j, j).wait_send()
        other = j + 1 - 2 * core
        relay(other, other).wait_recv()

    def dp_end(k):
        d = lax.rem(dp_me + k, dp_count)
        across(d, d).wait_send()
        beside(d, core).wait_send()

    loop(1, dp_count, dp_end)
    reverse.drain()
    forward.drain()
    loop(1, group + 1, lambda k: half(lax.rem(mine + k, group)).wait_send())
    loop(1, group, lambda k: scatter(lax.rem(mine + k, group), 0).wait_send())
    loop(1, seq_count, lambda k: tell(lax.rem(seq_me + k, seq_count), seq_me).wait_send())
    loop(1, seq_count // 2, end)
    loop(0, seq_count // 2, relayed)


def dma(*sizes):
    return [pltpu.SemaphoreType.DMA((size,)) for size in sizes for _ in range(2)]


def adam_update(grad_rows, weight_rows, first_rows, second_rows):
    new_first = beta_one * first_rows + (1.0 - beta_one) * grad_rows
    new_second = beta_two * second_rows + (1.0 - beta_two) * grad_rows * grad_rows
    first_hat = new_first / (1.0 - beta_one**adam_count)
    second_hat = new_second / (1.0 - beta_two**adam_count)
    new_weight = weight_rows - learn_rate * (
        first_hat / (jnp.sqrt(second_hat) + epsilon) + weight_decay * weight_rows
    )
    return (new_weight, new_first, new_second)


def on_device(
    layer_input,
    scan_input,
    readout,
    log_decay,
    output_cotangent,
    write_weight,
    first_moment,
    second_moment,
):
    seq_count, dp_count = lax.axis_size("seq"), lax.axis_size("dp")
    input_rows = layer_input[0]
    scan_rows = scan_input[0]
    read_rows = readout[0]
    decay_rows = log_decay[0]
    back_rows = output_cotangent[0]
    length, model = input_rows.shape
    heads = decay_rows.shape[1]
    channels = scan_rows.shape[1]
    state_size = read_rows.shape[1]
    own_rows = write_weight.shape[0]
    width = channels // seq_count

    chips = seq_count // 2
    group = chips * dp_count
    if own_rows % (128 * seq_count) == 0:
        piece = (state_size, own_rows // seq_count)
        exchange = [pltpu.VMEM((seq_count, state_size, width), bf16)] * 2
        exact_exchange = [pltpu.VMEM((seq_count, state_size, width), d) for d in (bf16, f32)]
        states = pltpu.VMEM((state_size, channels), bf16)
        exact_states = pltpu.VMEM((state_size, channels), f32)
        halves = (2, state_size // 2, own_rows)
        decay_grad, grad_sum = pl.pallas_call(
            functools.partial(one_kernel, seq_count, dp_count),
            out_shape=(
                jax.ShapeDtypeStruct((heads, length), f32),
                jax.ShapeDtypeStruct((seq_count,) + piece, bf16),
            ),
            in_specs=[VMEM] * 6,
            out_specs=[VMEM] * 2,
            scratch_shapes=[
                states,
                exact_states,
                pltpu.VMEM(halves, bf16),
                states,
                pltpu.VMEM((seq_count, 1, width), f32),
                pltpu.VMEM((length, channels), f32),
                pltpu.VMEM((heads, length, length), f32),
                pltpu.VMEM((length, heads), f32),
                pltpu.VMEM((heads, length), f32),
                pltpu.VMEM((dp_count,) + halves, bf16),
                pltpu.VMEM((seq_count, 1, width), f32),
                states,
            ]
            + exchange
            + exact_exchange
            + [pltpu.VMEM((2, group) + piece, bf16)]
            + [pltpu.VMEM((group,) + piece, bf16)] * 3
            + dma(dp_count, dp_count, seq_count, seq_count, seq_count, seq_count, seq_count,
                  group, group, seq_count, seq_count),
            compiler_params=pltpu.CompilerParams(collective_id=3, has_side_effects=True),
            name="whole_step",
        )(write_weight.T, decay_rows.T, scan_rows, back_rows, read_rows.T, input_rows)
        decay_grad = decay_grad.T
    else:
        running = jnp.cumsum(decay_rows, axis=0)
        overall = running[-1]
        to_end = jnp.exp(overall[None, :] - running)
        from_start = jnp.exp(running)
        decay_total = jnp.exp(overall)

        def widen(a):
            return jnp.repeat(a, HEAD_DIM, axis=1)

        scaled_scan = scan_rows.astype(f32) * widen(to_end)
        scaled_back = back_rows.astype(f32) * widen(from_start)

        def state_of(vectors, rows):
            return lax.dot_general(
                vectors.astype(f32), rows, (((0,), (0,)), ((), ())), precision=highest
            )

        reverse_local = state_of(read_rows, scaled_back).astype(bf16)
        decay_lanes = widen(decay_total[None]).reshape(seq_count, 1, width)
        weight_half = write_weight.T.astype(bf16).reshape(2, state_size // 2, own_rows)
        exchange = [
            pltpu.VMEM((seq_count, state_size, width), bf16),
            pltpu.VMEM((seq_count, state_size, width), bf16),
        ]
        piece = (state_size * own_rows // seq_count // 128, 128)
        scan_split = scan_rows.reshape(length, heads, HEAD_DIM)
        back_split = back_rows.reshape(length, heads, HEAD_DIM)
        crossed = jnp.einsum("thp,shp->hts", scan_split, back_split, preferred_element_type=f32)
        heads_running = running.T
        spread = heads_running[:, None, :] - heads_running[:, :, None]
        row_index = lax.broadcasted_iota(jnp.int32, (length, length), 0)
        col_index = lax.broadcasted_iota(jnp.int32, (length, length), 1)
        kernel_mat = (
            jnp.where((row_index <= col_index)[None], jnp.exp(jnp.minimum(spread, 0.0)), 0.0) * crossed
        )
        weights, decays, grad_after = pl.pallas_call(
            functools.partial(first_kernel, seq_count, dp_count),
            out_shape=(
                jax.ShapeDtypeStruct((dp_count,) + weight_half.shape, bf16),
                jax.ShapeDtypeStruct(decay_lanes.shape, f32),
                jax.ShapeDtypeStruct((state_size, channels), bf16),
            ),
            in_specs=[VMEM] * 3,
            out_specs=[VMEM] * 3,
            scratch_shapes=exchange + dma(dp_count, dp_count, seq_count, seq_count, seq_count),
            compiler_params=pltpu.CompilerParams(collective_id=0, has_side_effects=True),
            name="gather_reverse",
        )(weight_half, reverse_local, decay_lanes)

        weight_all = weights.reshape(dp_count, state_size, own_rows).transpose(1, 0, 2)
        write_half = lax.dot_general(
            input_rows, weight_all.reshape(state_size, model), (((1,), (1,)), ((), ())),
            preferred_element_type=f32,
        ).astype(bf16)
        state_local = state_of(write_half, scaled_scan)
        state_before = pl.pallas_call(
            functools.partial(second_kernel, seq_count),
            out_shape=jax.ShapeDtypeStruct((state_size, channels), f32),
            in_specs=[VMEM] * 2,
            out_specs=VMEM,
            scratch_shapes=[pltpu.VMEM((seq_count, state_size, width), f32)] * 2 + dma(seq_count, seq_count),
            compiler_params=pltpu.CompilerParams(collective_id=1, has_side_effects=True),
            name="forward_states",
        )(state_local, decays)

        kernel_sum = jnp.sum(kernel_mat, axis=0)
        write_grad = jnp.dot(kernel_sum, read_rows.astype(f32), precision=highest)
        write_grad = write_grad + lax.dot_general(
            scaled_scan.astype(bf16), grad_after, (((1,), (1,)), ((), ())), preferred_element_type=f32
        )
        grad_half = write_grad.astype(bf16)
        partial = lax.dot_general(
            grad_half, input_rows, (((0,), (0,)), ((), ())), preferred_element_type=f32
        ).astype(bf16)
        part = partial.reshape(state_size, dp_count, chips, 2, own_rows // seq_count)
        part = part.transpose(3, 2, 1, 0, 4).reshape((2, chips * dp_count) + piece)
        grad_sum = pl.pallas_call(
            functools.partial(third_kernel, seq_count, dp_count),
            out_shape=jax.ShapeDtypeStruct((seq_count,) + piece, bf16),
            in_specs=[VMEM],
            out_specs=VMEM,
            scratch_shapes=[pltpu.VMEM((chips * dp_count,) + piece, bf16)] * 3
            + dma(chips * dp_count, chips * dp_count, seq_count),
            compiler_params=pltpu.CompilerParams(collective_id=2, has_side_effects=True),
            name="reduce_gradient",
        )(part)
        def per_head(a):
            return jnp.sum(a.reshape(a.shape[0], heads, HEAD_DIM), axis=2)

        term_one = decay_total * jnp.sum(
            per_head(grad_after.astype(f32) * state_before.astype(f32)), axis=0)
        grad_write = jnp.dot(write_half, grad_after, preferred_element_type=f32)
        second_rows = to_end * per_head(scan_rows.astype(f32) * grad_write)
        term_two = jnp.cumsum(second_rows, axis=0) - second_rows
        state_read = jnp.dot(read_rows.astype(f32), state_before, precision=highest)
        third_rows = from_start * per_head(back_rows.astype(f32) * state_read)
        term_three = jnp.flip(jnp.cumsum(jnp.flip(third_rows, 0), axis=0), 0)
        write_read = jnp.dot(write_half, read_rows.T, preferred_element_type=f32)
        pairing = jnp.where((row_index < col_index)[None], kernel_mat * write_read[None], 0.0)
        balance = (jnp.sum(pairing, axis=2) - jnp.sum(pairing, axis=1)).T
        term_four = jnp.cumsum(balance, axis=0) - balance
        decay_grad = term_one[None, :] + term_two + term_three + term_four
    grad_rows = grad_sum.reshape(seq_count, state_size, own_rows // seq_count).transpose(1, 0, 2)
    grad_rows = grad_rows.reshape(state_size, own_rows).astype(f32).T
    new_weight, new_first, new_second = adam_update(
        grad_rows, write_weight, first_moment, second_moment
    )

    return (decay_grad[None], new_weight, new_first, new_second)


def solution(mesh):
    in_specs = (
        P("dp", "seq", None),
        P("dp", "seq", None),
        P("dp", "seq", None),
        P("dp", "seq", None),
        P("dp", "seq", None),
        P("dp", None),
        P("dp", None),
        P("dp", None),
    )
    out_specs = (P("dp", "seq", None), P("dp", None), P("dp", None), P("dp", None))
    return jax.shard_map(
        on_device, mesh=mesh, in_specs=in_specs, out_specs=out_specs, check_vma=False
    )
```
